128 devices in a mesh: ctx: 8 (over z, x_hi), fsdp: 16 (over y, x_lo, core).
Axes of the slice: x: 4 (x_hi: 2, x_lo: 2; x = x_hi * 2 + x_lo), y: 4, z: 4, core: 2. Of those that a mesh axis runs over, the one named last changes fastest.
Arguments:
- queries: bfloat16 [16, 2048, 2048], P('fsdp', 'ctx'), may hold values from -36 to 36
- keys: bfloat16 [16, 2048, 512], P('fsdp', 'ctx'), may hold values from -6 to 6
- values: bfloat16 [16, 2048, 512], P('fsdp', 'ctx'), may hold values from -6 to 6
- resid: bfloat16 [16, 2048, 2048], P('fsdp', 'ctx'), may hold values from -6 to 6
- grad_out: bfloat16 [16, 2048, 2048], P('fsdp', 'ctx'), may hold values from -8 to 8
- w_out: bfloat16 [2048, 2048], P(None, 'fsdp'), may hold values from -0.125 to 0.125
- block_list: int32 [16, 8], P('ctx'), may hold values from 0 to 15, as said below
- block_count: int32 [16], P('ctx'), may hold values from 1 to 8, as said below
Outputs:
- mixed: bfloat16 [16, 2048, 2048], P('fsdp', 'ctx')
- query_grad: bfloat16 [16, 2048, 2048], P('fsdp', 'ctx')
- key_grad: bfloat16 [16, 2048, 512], P('fsdp', 'ctx')
- value_grad: bfloat16 [16, 2048, 512], P('fsdp', 'ctx')
- proj_grad: float32 [2048, 2048], P('ctx', 'fsdp')
The draws below stay inside these ranges and needn't reach their ends.
Inputs may be any that keep to these rules, and one draw needn't show every extreme that they name: `block_list`: row r lists the key blocks of query block r within its sequence: entry 0 is r itself; entries 1 to block_count[r] - 1 are distinct blocks before r; entries from block_count[r] on are ignored and hold r or earlier blocks. block_count[r] is at most min(r + 1, 8); the last query block has exactly 8.
All inputs are finite; a program needn't handle non-finite values.
Results may differ from the reference program's by a relative error of at most 0.025.
Values may be sent and summed in bfloat16 or wider, within the bound.
A program may use at most 192 MiB of HBM per device.

```python
import math
import jax
import jax.numpy as jnp
from jax import lax

D = 2048
QUERY_HEADS = 16
KEY_VALUE_HEADS = 4
HEAD_DIM = 128
BLOCK_SIZE = 128
KEY_SLOTS = 8
SEQ_LENGTH = 2048
BLOCKS_PER_SEQ = 16
SEQUENCE_COUNT = 16
N_CTX = 8


def query_key_pair(key):
    base = jax.random.fold_in(key, 7)
    query_key, key_random_seed = jax.random.split(base, 2)
    query_sample = jnp.clip(jax.random.normal(query_key, (SEQUENCE_COUNT, SEQ_LENGTH, QUERY_HEADS, HEAD_DIM), jnp.float32), -6.0, 6.0)
    key_sample = jnp.clip(jax.random.normal(key_random_seed, (SEQUENCE_COUNT, SEQ_LENGTH, KEY_VALUE_HEADS, HEAD_DIM), jnp.float32), -6.0, 6.0)
    return (query_sample.reshape(SEQUENCE_COUNT, SEQ_LENGTH, QUERY_HEADS * HEAD_DIM), key_sample.reshape(SEQUENCE_COUNT, SEQ_LENGTH, KEY_VALUE_HEADS * HEAD_DIM))


def draw_queries(key, part):
    return query_key_pair(key)[0].astype(jnp.bfloat16)


def draw_keys(key, part):
    return query_key_pair(key)[1].astype(jnp.bfloat16)


def block_pattern(key):
    base = jax.random.fold_in(key, 11)
    count_key, order_key = jax.random.split(base)
    block_ids = jnp.arange(BLOCKS_PER_SEQ, dtype=jnp.int32)
    limit = jnp.minimum(block_ids + 1, KEY_SLOTS)
    counts = jax.random.randint(count_key, (BLOCKS_PER_SEQ,), 0, 1 << 20, jnp.int32) % limit + 1
    counts = jnp.where(block_ids == BLOCKS_PER_SEQ - 1, KEY_SLOTS, counts).astype(jnp.int32)
    ranks = jax.random.randint(order_key, (BLOCKS_PER_SEQ, BLOCKS_PER_SEQ), 0, 1 << 16, jnp.int32) * BLOCKS_PER_SEQ + block_ids[None, :]
    earlier = block_ids[None, :] < block_ids[:, None]
    ranks = jnp.where(earlier, ranks, -1 - block_ids[None, :])
    ordered = jnp.argsort(-ranks, axis=1, stable=True).astype(jnp.int32)
    chosen = ordered[:, :KEY_SLOTS - 1]
    usable = jnp.arange(KEY_SLOTS - 1, dtype=jnp.int32)[None, :] < block_ids[:, None]
    chosen = jnp.where(usable, chosen, block_ids[:, None])
    listing = jnp.concatenate([block_ids[:, None], chosen], axis=1).astype(jnp.int32)
    return (listing, counts)


def draw_block_list(key, part):
    return block_pattern(key)[0]


def draw_block_count(key, part):
    return block_pattern(key)[1]


def with_spikes(result, stream_key, source, target, blocks, factor):
    owner, partner = [(jnp.arange(result.shape[axis_at]) // (result.shape[axis_at] // blocks)).reshape([-1 if axis == axis_at else 1 for axis in range(result.ndim)]) for axis_at in (source, target)]
    chosen = jax.random.permutation(stream_key, blocks)[partner]
    strong = (owner == chosen) | (owner == (partner + blocks // 2) % blocks)
    return jnp.where(strong, factor * result, result)


def level_of(stream_key, dims, cuts, low, largest):
    def one(dim, parts):
        heights = jax.random.uniform(jax.random.fold_in(jax.random.fold_in(stream_key, 6), dim), (parts,), jnp.float32, low / len(cuts), largest / len(cuts))
        return jnp.repeat(jnp.exp(heights), dims[dim] // parts).reshape((-1,) + (1,) * (len(dims) - dim - 1))

    level = one(*cuts[0])
    for cut in cuts[1:]:
        level = level * one(*cut)
    return level


def scatter_about(key, shape, spread, reach, pieces=(), held_as=jnp.bfloat16):
    values = spread * jax.random.normal(key, shape, jnp.float32)
    if pieces:
        values = values * level_of(key, shape, pieces, -0.22, 0.18)
    return jnp.clip(values, -reach, reach).astype(held_as)


def heavy_noise(stream_key, dims, spread, reach, cuts, heavy, kind=jnp.bfloat16):
    array = spread * jax.random.normal(stream_key, dims, jnp.float32)
    if cuts:
        array = array * level_of(stream_key, dims, cuts, -0.22, 0.18)
    return jnp.clip(with_spikes(array, jax.random.fold_in(stream_key, 3), *heavy), -reach, reach).astype(kind)


def setup_inputs(seed: int = 0) -> dict:
    key_list = jax.random.split(jax.random.key(seed), 9)
    queries = draw_queries(jax.random.fold_in(key_list[8], 71), 0)
    keys = draw_keys(jax.random.fold_in(key_list[8], 71), 0)
    values = scatter_about(key_list[2], (SEQUENCE_COUNT, SEQ_LENGTH, KEY_VALUE_HEADS * HEAD_DIM), 1.0, 6.0, ((0, 16), (1, 8)))
    resid = scatter_about(key_list[3], (SEQUENCE_COUNT, SEQ_LENGTH, D), 1.0, 6.0, ((0, 16), (1, 8)))
    grad_out = heavy_noise(key_list[4], (SEQUENCE_COUNT, SEQ_LENGTH, D), 1.0, 8.0, ((0, 16), (1, 8)), (0, 2, 16, 2.0))
    w_out = scatter_about(key_list[5], (QUERY_HEADS * HEAD_DIM, D), (QUERY_HEADS * HEAD_DIM) ** -0.5, 0.125, ((1, 16),))
    block_list = draw_block_list(jax.random.fold_in(key_list[8], 71), 0)
    block_count = draw_block_count(jax.random.fold_in(key_list[8], 71), 0)
    return dict(queries=queries, keys=keys, values=values, resid=resid, grad_out=grad_out, w_out=w_out, block_list=block_list, block_count=block_count)


def score_mask(first_row, listed_blocks, live_count):
    query_pos = first_row + jnp.arange(BLOCK_SIZE, dtype=jnp.int32)
    key_pos = listed_blocks[:, None] * BLOCK_SIZE + jnp.arange(BLOCK_SIZE, dtype=jnp.int32)[None, :]
    slot_live = jnp.arange(KEY_SLOTS, dtype=jnp.int32) < live_count
    return (key_pos[None, :, :] <= query_pos[:, None, None]) & slot_live[None, :, None]

def block_weights(query_blk, key_sel, allowed):
    scale = 1.0 / math.sqrt(HEAD_DIM)
    scores = jnp.einsum('qgrd,sbgd->grqsb', query_blk.astype(jnp.float32), key_sel.astype(jnp.float32)) * scale
    scores = jnp.where(allowed[None, None], scores, jnp.float32(-1e+30))
    top = lax.optimization_barrier(jnp.max(scores, axis=(3, 4), keepdims=True))
    expon = jnp.exp(scores - top)
    probs = expon / lax.optimization_barrier(jnp.sum(expon, axis=(3, 4), keepdims=True))
    return (probs, probs.astype(jnp.bfloat16))

def reference(queries, keys, values, resid, grad_out, w_out, block_list, block_count):
    scale = 1.0 / math.sqrt(HEAD_DIM)
    query_groups = QUERY_HEADS // KEY_VALUE_HEADS
    positions = jnp.arange(BLOCKS_PER_SEQ, dtype=jnp.int32)

    def one_sequence(operands):
        query_sequence, key_sequence, value_sequence, resid_seq, grad_seq = operands
        blocked_keys = key_sequence.reshape(BLOCKS_PER_SEQ, BLOCK_SIZE, KEY_VALUE_HEADS, HEAD_DIM)
        blocked_values = value_sequence.reshape(BLOCKS_PER_SEQ, BLOCK_SIZE, KEY_VALUE_HEADS, HEAD_DIM)
        blocked_queries = query_sequence.reshape(BLOCKS_PER_SEQ, BLOCK_SIZE, KEY_VALUE_HEADS, query_groups, HEAD_DIM)

        def forward_block(block_pos):
            listed_blocks = block_list[block_pos]
            allowed = score_mask(block_pos * BLOCK_SIZE, listed_blocks, block_count[block_pos])
            key_sel = jnp.take(blocked_keys, listed_blocks, axis=0)
            value_sel = jnp.take(blocked_values, listed_blocks, axis=0)
            probs, probs_b = block_weights(blocked_queries[block_pos], key_sel, allowed)
            attended = jnp.einsum('grqsb,sbgd->qgrd', probs_b.astype(jnp.float32), value_sel.astype(jnp.float32))
            return attended.astype(jnp.bfloat16)
        out_blocks = lax.map(forward_block, positions)
        out_rows = out_blocks.reshape(SEQ_LENGTH, QUERY_HEADS * HEAD_DIM)
        mixed = (resid_seq.astype(jnp.float32) + jnp.dot(out_rows, w_out, preferred_element_type=jnp.float32)).astype(jnp.bfloat16)
        attended_gradient = lax.dot_general(grad_seq, w_out, (((1,), (1,)), ((), ())), preferred_element_type=jnp.float32).astype(jnp.bfloat16)
        output_grad_blocks = attended_gradient.reshape(BLOCKS_PER_SEQ, BLOCK_SIZE, KEY_VALUE_HEADS, query_groups, HEAD_DIM)

        def backward_block(block_pos):
            listed_blocks = block_list[block_pos]
            allowed = score_mask(block_pos * BLOCK_SIZE, listed_blocks, block_count[block_pos])
            key_sel = jnp.take(blocked_keys, listed_blocks, axis=0)
            value_sel = jnp.take(blocked_values, listed_blocks, axis=0)
            query_blk = blocked_queries[block_pos]
            dout_blk = output_grad_blocks[block_pos]
            probs, probs_b = block_weights(query_blk, key_sel, allowed)
            value_part = jnp.einsum('grqsb,qgrd->sbgd', probs_b.astype(jnp.float32), dout_blk.astype(jnp.float32))
            prob_grads = jnp.einsum('qgrd,sbgd->grqsb', dout_blk.astype(jnp.float32), value_sel.astype(jnp.float32))
            row_dot = lax.optimization_barrier(jnp.sum(dout_blk.astype(jnp.float32) * out_blocks[block_pos].astype(jnp.float32), axis=-1))
            row_dot = jnp.transpose(row_dot, (1, 2, 0))[:, :, :, None, None]
            score_grads = (probs * (prob_grads - row_dot) * scale).astype(jnp.bfloat16)
            query_part = jnp.einsum('grqsb,sbgd->qgrd', score_grads.astype(jnp.float32), key_sel.astype(jnp.float32)).astype(jnp.bfloat16)
            key_part = jnp.einsum('grqsb,qgrd->sbgd', score_grads.astype(jnp.float32), query_blk.astype(jnp.float32))
            return (query_part, key_part, value_part)
        query_parts, key_fragments, value_fragments = lax.map(backward_block, positions)
        slice_blocks = BLOCKS_PER_SEQ // N_CTX

        def shard_partial(shard):
            start_index = (shard * slice_blocks).astype(jnp.int32)
            listed_blocks = lax.dynamic_slice_in_dim(block_list, start_index, slice_blocks, 0).reshape(-1)
            key_fragment = lax.dynamic_slice_in_dim(key_fragments, start_index, slice_blocks, 0).reshape(slice_blocks * KEY_SLOTS, BLOCK_SIZE, KEY_VALUE_HEADS * HEAD_DIM)
            value_fragment = lax.dynamic_slice_in_dim(value_fragments, start_index, slice_blocks, 0).reshape(slice_blocks * KEY_SLOTS, BLOCK_SIZE, KEY_VALUE_HEADS * HEAD_DIM)
            key_holder = jnp.zeros((BLOCKS_PER_SEQ, BLOCK_SIZE, KEY_VALUE_HEADS * HEAD_DIM), jnp.float32).at[listed_blocks].add(key_fragment)
            value_holder = jnp.zeros((BLOCKS_PER_SEQ, BLOCK_SIZE, KEY_VALUE_HEADS * HEAD_DIM), jnp.float32).at[listed_blocks].add(value_fragment)
            return (key_holder.astype(jnp.bfloat16), value_holder.astype(jnp.bfloat16))
        key_slices, value_slices = lax.map(shard_partial, jnp.arange(N_CTX, dtype=jnp.int32))
        key_gradient_sum = lax.optimization_barrier(jnp.sum(key_slices.astype(jnp.float32), axis=0)).astype(jnp.bfloat16).reshape(SEQ_LENGTH, KEY_VALUE_HEADS * HEAD_DIM)
        value_gradient_sum = lax.optimization_barrier(jnp.sum(value_slices.astype(jnp.float32), axis=0)).astype(jnp.bfloat16).reshape(SEQ_LENGTH, KEY_VALUE_HEADS * HEAD_DIM)
        return (mixed, query_parts.reshape(SEQ_LENGTH, QUERY_HEADS * HEAD_DIM), key_gradient_sum, value_gradient_sum, out_rows)
    mixed, query_grad, key_grad, value_grad, attended = lax.map(one_sequence, (queries, keys, values, resid, grad_out))
    proj_grad = jnp.dot(attended.reshape(SEQUENCE_COUNT * SEQ_LENGTH, QUERY_HEADS * HEAD_DIM).T, grad_out.reshape(SEQUENCE_COUNT * SEQ_LENGTH, D), preferred_element_type=jnp.float32)
    return (mixed, query_grad, key_grad, value_grad, proj_grad)
```

```python
import math

import jax
import jax.numpy as jnp
from jax import lax
from jax.experimental import pallas as pl
from jax.experimental.pallas import tpu as pltpu
from jax.sharding import PartitionSpec as P

QUERY_HEADS = 16
KV_HEADS = 4
GROUP = QUERY_HEADS // KV_HEADS
HEAD_DIM = 128
BLOCK = 128
SLOTS = 8
SCALE = 1.0 / math.sqrt(HEAD_DIM)
BF16 = jnp.bfloat16
F32 = jnp.float32
MESH = pl.DeviceIdType.MESH


def dot(a, b, ca, cb):
    return lax.dot_general(a, b, (((ca,), (cb,)), ((), ())), preferred_element_type=F32)


def stack_heads(x):
    return jnp.concatenate(
        [x[:, h * HEAD_DIM : (h + 1) * HEAD_DIM] for h in range(GROUP)], axis=0
    )


def attention_kernel(
    list_ref, count_ref, q_ref, do_ref, k_ref, v_ref, att_ref, dq_ref, dk_ref, dv_ref, dk_acc, dv_acc
):
    i = pl.program_id(1)
    cols = GROUP * BLOCK

    @pl.when(i == 0)
    def _():
        dk_acc[...] = jnp.zeros_like(dk_acc)
        dv_acc[...] = jnp.zeros_like(dv_acc)

    q4 = stack_heads(q_ref[...])
    do4 = stack_heads(do_ref[...])
    live = count_ref[i]
    rows = [pl.ds(pl.multiple_of(list_ref[i, j] * BLOCK, BLOCK), BLOCK) for j in range(SLOTS)]
    k_sel = jnp.concatenate([k_ref[0, r, :] for r in rows], axis=0)
    v_sel = jnp.concatenate([v_ref[0, r, :] for r in rows], axis=0)
    s = dot(k_sel, q4, 1, 1)
    key_pos = lax.broadcasted_iota(jnp.int32, (BLOCK, cols), 0)
    query_pos = lax.broadcasted_iota(jnp.int32, (BLOCK, cols), 1) % BLOCK
    parts = [jnp.where(key_pos <= query_pos, s[:BLOCK], -1e30)]
    for j in range(1, SLOTS):
        bias = jnp.where(j < live, 0.0, -1e30).astype(F32)
        parts.append(s[j * BLOCK : (j + 1) * BLOCK] + bias)
    s = jnp.concatenate(parts, axis=0)
    top = jnp.max(s, axis=0, keepdims=True)
    e = jnp.exp((s - top) * SCALE)
    p = e * (1.0 / jnp.sum(e, axis=0, keepdims=True))
    pb = p.astype(BF16)
    o_t = dot(v_sel, pb, 0, 0)
    o4 = o_t.T.astype(BF16)
    row_dot = jnp.sum(o4.astype(F32) * do4.astype(F32), axis=1, keepdims=True)
    row_dot = jnp.broadcast_to(row_dot, (cols, HEAD_DIM)).T[:1]
    dp = dot(v_sel, do4, 1, 1)
    ds = (p * (dp - row_dot) * SCALE).astype(BF16)
    dq4 = dot(k_sel, ds, 0, 0).T.astype(BF16)
    dk_sel = dot(ds, q4, 1, 0)
    dv_sel = dot(pb, do4, 1, 0)
    for h in range(GROUP):
        att_ref[:, h * HEAD_DIM : (h + 1) * HEAD_DIM] = o4[h * BLOCK : (h + 1) * BLOCK]
        dq_ref[:, h * HEAD_DIM : (h + 1) * HEAD_DIM] = dq4[h * BLOCK : (h + 1) * BLOCK]
    for j in range(SLOTS):
        dk_acc[rows[j], :] += dk_sel[j * BLOCK : (j + 1) * BLOCK]
        dv_acc[rows[j], :] += dv_sel[j * BLOCK : (j + 1) * BLOCK]

    @pl.when(i == pl.num_programs(1) - 1)
    def _():
        dk_ref[0] = dk_acc[...].astype(BF16)
        dv_ref[0] = dv_acc[...].astype(BF16)


def attention(queries, datt, kv, block_list, block_count):
    rows, width = queries.shape
    seq = kv.shape[1]
    group_cols = GROUP * HEAD_DIM
    kv_cols = KV_HEADS * HEAD_DIM
    q_spec = pl.BlockSpec((BLOCK, group_cols), lambda g, i, *_: (i, g))

    def kv_spec(which):
        return pl.BlockSpec((1, seq, HEAD_DIM), lambda g, i, *_: (which, 0, g))

    out_spec = pl.BlockSpec((1, seq, HEAD_DIM), lambda g, i, *_: (0, 0, g))
    flops = 12 * rows * QUERY_HEADS * SLOTS * BLOCK * HEAD_DIM
    return pl.pallas_call(
        attention_kernel,
        grid_spec=pltpu.PrefetchScalarGridSpec(
            num_scalar_prefetch=2,
            grid=(KV_HEADS, rows // BLOCK),
            in_specs=[q_spec, q_spec, kv_spec(0), kv_spec(1)],
            out_specs=[q_spec, q_spec, out_spec, out_spec],
            scratch_shapes=[pltpu.VMEM((seq, HEAD_DIM), F32)] * 2,
        ),
        out_shape=[
            jax.ShapeDtypeStruct((rows, width), BF16),
            jax.ShapeDtypeStruct((rows, width), BF16),
            jax.ShapeDtypeStruct((1, seq, kv_cols), BF16),
            jax.ShapeDtypeStruct((1, seq, kv_cols), BF16),
        ],
        compiler_params=pltpu.CompilerParams(
            dimension_semantics=("arbitrary", "arbitrary"), vmem_limit_bytes=48 << 20
        ),
        cost_estimate=pl.CostEstimate(
            flops=flops, bytes_accessed=12 << 20, transcendentals=rows * QUERY_HEADS * SLOTS * BLOCK
        ),
        name="attention",
    )(block_list, block_count, queries, datt, kv, kv)


def mesh_spot():
    c, f = lax.axis_index("ctx"), lax.axis_index("fsdp")
    return c, f, c // 2, lax.rem(c, 2), f // 4, lax.rem(f // 2, 2), lax.rem(f, 2)


def neighbours():
    c, f, z, xh, y, xl, k = mesh_spot()
    z_up, z_down = lax.rem(z + 1, 4), lax.rem(z + 3, 4)
    y_up, y_down = lax.rem(y + 1, 4), lax.rem(y + 3, 4)
    side, far, twin = 4 * y + 2 * (1 - xl) + k, 2 * z + 1 - xh, 4 * y + 2 * xl + 1 - k
    return dict(
        far=(far, f),
        near=(c, side),
        back=(far, side),
        twin=(c, twin),
        z_up=(2 * z_up + xh, f),
        z_down=(2 * z_down + xh, f),
        y_up=(c, 4 * y_up + 2 * xl + k),
        y_down=(c, 4 * y_down + 2 * xl + k),
    )


def meet(peers):
    barrier = pltpu.get_barrier_semaphore()
    for peer in peers:
        pl.semaphore_signal(barrier, inc=1, device_id=peer, device_id_type=MESH)
    pl.semaphore_wait(barrier, len(peers))


class Flows:
    def __init__(self, send_sem, recv_sem):
        self.send_sem, self.recv_sem, self.made = send_sem, recv_sem, []

    def send(self, src, dst, peer):
        n = len(self.made)
        copy = pltpu.make_async_remote_copy(
            src_ref=src,
            dst_ref=dst,
            send_sem=self.send_sem.at[n],
            recv_sem=self.recv_sem.at[n],
            device_id=peer,
            device_id_type=MESH,
        )
        copy.start()
        self.made.append(copy)
        return copy

    def finish(self):
        for copy in self.made:
            copy.wait_send()


GATHER_FLOWS = 40


def gather_kernel(
    keys, values, grad, w, kv, w_all, datt, w_buf, total, send_sem, recv_sem, here_sem
):
    c, f, z, xh, y, xl, k = mesh_spot()
    at = neighbours()
    z_up, z_down, z_far = lax.rem(z + 1, 4), lax.rem(z + 3, 4), lax.rem(z + 2, 4)
    y_up, y_down, y_far = lax.rem(y + 1, 4), lax.rem(y + 3, 4), lax.rem(y + 2, 4)
    rows = keys.shape[0]
    half = w.shape[0] // 2
    meet(list(at.values()))
    flows = Flows(send_sem, recv_sem)

    def chunk(a, who):
        return kv.at[a, pl.ds(pl.multiple_of(who * rows, rows), rows), :]

    def shard(yy, xx, kk):
        return 4 * yy + 2 * xx + kk

    def whole(who):
        return w_buf.at[who]

    def part(who, p):
        return w_buf.at[who, pl.ds(p * half, half), :]

    own = (keys, values)
    kv_far = [flows.send(own[a], chunk(a, c), at["far"]) for a in (0, 1)]
    kv_up = [flows.send(own[a], chunk(a, c), at["z_up"]) for a in (0, 1)]
    kv_down = [flows.send(own[a], chunk(a, c), at["z_down"]) for a in (1, 0)][::-1]
    w_up = flows.send(w, whole(f), at["y_up"])
    w_down = flows.send(w, whole(f), at["y_down"])
    w_side = [
        flows.send(w.at[pl.ds(p * half, half), :], part(f, p), at[("near", "back")[p]])
        for p in (0, 1)
    ]
    to_twin = [flows.send(w, whole(f), at["twin"])]
    here = [
        pltpu.make_async_copy(keys, chunk(0, c), here_sem.at[0]),
        pltpu.make_async_copy(values, chunk(1, c), here_sem.at[1]),
        pltpu.make_async_copy(w, whole(f), here_sem.at[2]),
    ]
    for copy in here:
        copy.start()

    kv_up[0].wait_recv()
    on_k = flows.send(chunk(0, 2 * z_down + xh), chunk(0, 2 * z_down + xh), at["z_up"])
    kv_down[1].wait_recv()
    on_v = flows.send(chunk(1, 2 * z_up + xh), chunk(1, 2 * z_up + xh), at["z_down"])
    w_up.wait_recv()
    got = shard(y_down, xl, k)
    on_w0 = flows.send(part(got, 0), part(got, 0), at["y_up"])
    to_twin.append(flows.send(whole(got), whole(got), at["twin"]))
    w_down.wait_recv()
    got = shard(y_up, xl, k)
    on_w1 = flows.send(part(got, 1), part(got, 1), at["y_down"])
    to_twin.append(flows.send(whole(got), whole(got), at["twin"]))

    other = 2 * z + 1 - xh
    side = shard(y, 1 - xl, k)
    pair_up, pair_down = [None, None], [None, None]
    for a in (0, 1):
        kv_far[a].wait_recv()
        pair_up[a] = flows.send(chunk(a, other), chunk(a, other), at["z_up"])
        pair_down[a] = flows.send(chunk(a, other), chunk(a, other), at["z_down"])
    side_up, side_down = [], []
    for p in (0, 1):
        w_side[p].wait_recv()
        side_up.append(flows.send(part(side, p), part(side, p), at["y_up"]))
        side_down.append(flows.send(part(side, p), part(side, p), at["y_down"]))
    to_twin.append(flows.send(whole(side), whole(side), at["twin"]))

    def multiply(yy, first):
        def columns(n, carry):
            lanes = pl.ds(pl.multiple_of(n * 512, 512), 512)
            out = None
            for s in range(4):
                who = 4 * yy + s
                g = grad[:, pl.ds(pl.multiple_of(who * HEAD_DIM, HEAD_DIM), HEAD_DIM)]
                term = dot(g, w_buf[who, lanes, :], 1, 1)
                out = term if out is None else out + term
            total[:, lanes] = out if first else total[:, lanes] + out
            return carry

        lax.fori_loop(0, total.shape[1] // 512, columns, 0)

    kv_up[1].wait_recv()
    kv_down[0].wait_recv()
    got = shard(y_down, 1 - xl, k)
    side_up[0].wait_recv()
    on_s0 = flows.send(part(got, 0), part(got, 0), at["y_up"])
    side_up[1].wait_recv()
    to_twin.append(flows.send(whole(got), whole(got), at["twin"]))
    got = shard(y_up, 1 - xl, k)
    side_down[0].wait_recv()
    side_down[1].wait_recv()
    on_s1 = flows.send(part(got, 1), part(got, 1), at["y_down"])
    to_twin.append(flows.send(whole(got), whole(got), at["twin"]))

    pair_up[0].wait_recv()
    got = 2 * z_down + 1 - xh
    pair_on_k = flows.send(chunk(0, got), chunk(0, got), at["z_up"])
    pair_down[1].wait_recv()
    got = 2 * z_up + 1 - xh
    pair_on_v = flows.send(chunk(1, got), chunk(1, got), at["z_down"])

    got = shard(y_far, xl, k)
    on_w0.wait_recv()
    to_twin.append(flows.send(part(got, 0), part(got, 0), at["twin"]))
    on_w1.wait_recv()
    to_twin.append(flows.send(part(got, 1), part(got, 1), at["twin"]))
    for copy in here:
        copy.wait()
    for n in (0, 3):
        to_twin[n].wait_recv()
    multiply(y, True)
    for n in (1, 4):
        to_twin[n].wait_recv()
    multiply(y_down, False)
    for n in (2, 5):
        to_twin[n].wait_recv()
    multiply(y_up, False)

    got = shard(y_far, 1 - xl, k)
    on_s0.wait_recv()
    to_twin.append(flows.send(part(got, 0), part(got, 0), at["twin"]))
    on_s1.wait_recv()
    to_twin.append(flows.send(part(got, 1), part(got, 1), at["twin"]))
    for n in (6, 7, 8, 9):
        to_twin[n].wait_recv()
    multiply(y_far, False)
    out = pltpu.make_async_copy(w_buf, w_all, here_sem.at[3])
    out.start()
    datt[...] = total[...].astype(BF16)
    on_k.wait_recv()
    on_v.wait_recv()
    pair_up[1].wait_recv()
    pair_down[0].wait_recv()
    pair_on_k.wait_recv()
    pair_on_v.wait_recv()
    flows.finish()
    out.wait()


def gather(keys, values, grad, w):
    rows, kv_cols = keys.shape
    feats, cols = w.shape
    n_ctx, n_fsdp = lax.axis_size("ctx"), lax.axis_size("fsdp")
    hbm = pl.BlockSpec(memory_space=pltpu.HBM)
    vmem = pl.BlockSpec(memory_space=pltpu.VMEM)
    return pl.pallas_call(
        gather_kernel,
        in_specs=[hbm, hbm, vmem, hbm],
        out_specs=[hbm, hbm, vmem],
        out_shape=[
            jax.ShapeDtypeStruct((2, n_ctx * rows, kv_cols), BF16),
            jax.ShapeDtypeStruct((n_fsdp, feats, cols), BF16),
            jax.ShapeDtypeStruct((rows, feats), BF16),
        ],
        scratch_shapes=[
            pltpu.VMEM((n_fsdp, feats, cols), BF16),
            pltpu.VMEM((rows, feats), F32),
            pltpu.SemaphoreType.DMA((GATHER_FLOWS,)),
            pltpu.SemaphoreType.DMA((GATHER_FLOWS,)),
            pltpu.SemaphoreType.DMA((4,)),
        ],
        compiler_params=pltpu.CompilerParams(
            collective_id=0, has_side_effects=True, vmem_limit_bytes=40 << 20
        ),
        cost_estimate=pl.CostEstimate(
            flops=2 * rows * feats * feats, bytes_accessed=24 << 20, transcendentals=0
        ),
        name="gather",
    )(keys, values, grad, w)


def local(queries, keys, values, resid, grad_out, w_out, block_list, block_count):
    grad_rows = grad_out[0]
    kv, w_all, datt = gather(keys[0], values[0], grad_rows, w_out)
    w_whole = w_all.transpose(1, 0, 2).reshape(w_out.shape[0], -1)
    att, dq, dk, dv = attention(queries[0], datt, kv, block_list, block_count)
    feature_share = lax.psum_scatter(
        lax.dot_general(
            grad_rows, att, (((0,), (0,)), ((), ())), preferred_element_type=F32
        ).astype(BF16),
        "fsdp",
        scatter_dimension=0,
        tiled=True,
    )
    dkv = lax.psum_scatter(
        jnp.concatenate([dk, dv], axis=0), "ctx", scatter_dimension=1, tiled=True
    )
    mixed = (resid[0].astype(F32) + jnp.dot(att, w_whole, preferred_element_type=F32)).astype(BF16)
    proj = lax.psum_scatter(feature_share, "ctx", scatter_dimension=1, tiled=True).astype(F32).T
    return mixed[None], dq[None], dkv[:1], dkv[1:], proj


def solution(mesh):
    rows = P("fsdp", "ctx", None)
    in_specs = (rows, rows, rows, rows, rows, P(None, "fsdp"), P("ctx", None), P("ctx"))
    out_specs = (rows, rows, rows, rows, P("ctx", "fsdp"))
    return jax.shard_map(local, mesh=mesh, in_specs=in_specs, out_specs=out_specs, check_vma=False)
```

```python
import math

import jax
import jax.numpy as jnp
from jax import lax
from jax.experimental import pallas as pl
from jax.experimental.pallas import tpu as pltpu
from jax.sharding import PartitionSpec as P

QUERY_HEADS = 16
KV_HEADS = 4
GROUP = QUERY_HEADS // KV_HEADS
HEAD_DIM = 128
BLOCK = 128
SLOTS = 8
SCALE = 1.0 / math.sqrt(HEAD_DIM)
BF16 = jnp.bfloat16
F32 = jnp.float32
MESH = pl.DeviceIdType.MESH


def dot(a, b, ca, cb):
    return lax.dot_general(a, b, (((ca,), (cb,)), ((), ())), preferred_element_type=F32)


def stack_heads(x):
    return jnp.concatenate(
        [x[:, h * HEAD_DIM : (h + 1) * HEAD_DIM] for h in range(GROUP)], axis=0
    )


def attention_kernel(
    list_ref, count_ref, q_ref, do_ref, k_ref, v_ref, att_ref, att_t_ref, dq_ref, dk_ref, dv_ref, dk_acc, dv_acc
):
    i = pl.program_id(1)
    cols = GROUP * BLOCK

    @pl.when(i == 0)
    def _():
        dk_acc[...] = jnp.zeros_like(dk_acc)
        dv_acc[...] = jnp.zeros_like(dv_acc)

    q4 = stack_heads(q_ref[...])
    do4 = stack_heads(do_ref[...])
    live = count_ref[i]
    rows = [pl.ds(pl.multiple_of(list_ref[i, j] * BLOCK, BLOCK), BLOCK) for j in range(SLOTS)]
    k_sel = jnp.concatenate([k_ref[0, r, :] for r in rows], axis=0)
    v_sel = jnp.concatenate([v_ref[0, r, :] for r in rows], axis=0)
    s = dot(k_sel, q4, 1, 1)
    key_pos = lax.broadcasted_iota(jnp.int32, (BLOCK, cols), 0)
    query_pos = lax.broadcasted_iota(jnp.int32, (BLOCK, cols), 1) % BLOCK
    parts = [jnp.where(key_pos <= query_pos, s[:BLOCK], -1e30)]
    for j in range(1, SLOTS):
        bias = jnp.where(j < live, 0.0, -1e30).astype(F32)
        parts.append(s[j * BLOCK : (j + 1) * BLOCK] + bias)
    s = jnp.concatenate(parts, axis=0)
    top = jnp.max(s, axis=0, keepdims=True)
    e = jnp.exp((s - top) * SCALE)
    p = e * (1.0 / jnp.sum(e, axis=0, keepdims=True))
    pb = p.astype(BF16)
    o_t = dot(v_sel, pb, 0, 0)
    o4 = o_t.T.astype(BF16)
    row_dot = jnp.sum(o4.astype(F32) * do4.astype(F32), axis=1, keepdims=True)
    row_dot = jnp.broadcast_to(row_dot, (cols, HEAD_DIM)).T[:1]
    dp = dot(v_sel, do4, 1, 1)
    ds = (p * (dp - row_dot) * SCALE).astype(BF16)
    dq4 = dot(k_sel, ds, 0, 0).T.astype(BF16)
    dk_sel = dot(ds, q4, 1, 0)
    dv_sel = dot(pb, do4, 1, 0)
    for h in range(GROUP):
        att_ref[:, h * HEAD_DIM : (h + 1) * HEAD_DIM] = o4[h * BLOCK : (h + 1) * BLOCK]
        att_t_ref[h] = o_t[:, h * BLOCK : (h + 1) * BLOCK].astype(BF16)
        dq_ref[:, h * HEAD_DIM : (h + 1) * HEAD_DIM] = dq4[h * BLOCK : (h + 1) * BLOCK]
    for j in range(SLOTS):
        dk_acc[rows[j], :] += dk_sel[j * BLOCK : (j + 1) * BLOCK]
        dv_acc[rows[j], :] += dv_sel[j * BLOCK : (j + 1) * BLOCK]

    @pl.when(i == pl.num_programs(1) - 1)
    def _():
        dk_ref[...] = dk_acc[...].astype(BF16)
        dv_ref[...] = dv_acc[...].astype(BF16)


def attention(queries, datt, kv, block_list, block_count):
    rows, width = queries.shape
    seq = kv.shape[1]
    group_cols = GROUP * HEAD_DIM
    kv_cols = KV_HEADS * HEAD_DIM
    q_spec = pl.BlockSpec((BLOCK, group_cols), lambda g, i, *_: (i, g))

    def kv_spec(which):
        return pl.BlockSpec((1, seq, HEAD_DIM), lambda g, i, *_: (which, 0, g))

    out_spec = pl.BlockSpec((seq, HEAD_DIM), lambda g, i, *_: (0, g))
    t_spec = pl.BlockSpec((GROUP, HEAD_DIM, BLOCK), lambda g, i, *_: (g, 0, i))
    flops = 12 * rows * QUERY_HEADS * SLOTS * BLOCK * HEAD_DIM
    return pl.pallas_call(
        attention_kernel,
        grid_spec=pltpu.PrefetchScalarGridSpec(
            num_scalar_prefetch=2,
            grid=(KV_HEADS, rows // BLOCK),
            in_specs=[q_spec, q_spec, kv_spec(0), kv_spec(1)],
            out_specs=[q_spec, t_spec, q_spec, out_spec, out_spec],
            scratch_shapes=[pltpu.VMEM((seq, HEAD_DIM), F32)] * 2,
        ),
        out_shape=[
            jax.ShapeDtypeStruct((rows, width), BF16),
            jax.ShapeDtypeStruct((QUERY_HEADS, HEAD_DIM, rows), BF16),
            jax.ShapeDtypeStruct((rows, width), BF16),
            jax.ShapeDtypeStruct((seq, kv_cols), BF16),
            jax.ShapeDtypeStruct((seq, kv_cols), BF16),
        ],
        compiler_params=pltpu.CompilerParams(
            dimension_semantics=("arbitrary", "arbitrary"), vmem_limit_bytes=48 << 20
        ),
        cost_estimate=pl.CostEstimate(
            flops=flops, bytes_accessed=12 << 20, transcendentals=rows * QUERY_HEADS * SLOTS * BLOCK
        ),
        name="attention",
    )(block_list, block_count, queries, datt, kv, kv)


def mesh_spot():
    c, f = lax.axis_index("ctx"), lax.axis_index("fsdp")
    return c, f, c // 2, lax.rem(c, 2), f // 4, lax.rem(f // 2, 2), lax.rem(f, 2)


def neighbours():
    c, f, z, xh, y, xl, k = mesh_spot()
    z_up, z_down = lax.rem(z + 1, 4), lax.rem(z + 3, 4)
    y_up, y_down = lax.rem(y + 1, 4), lax.rem(y + 3, 4)
    side, far, twin = 4 * y + 2 * (1 - xl) + k, 2 * z + 1 - xh, 4 * y + 2 * xl + 1 - k
    return dict(
        far=(far, f),
        near=(c, side),
        back=(far, side),
        twin=(c, twin),
        z_up=(2 * z_up + xh, f),
        z_down=(2 * z_down + xh, f),
        y_up=(c, 4 * y_up + 2 * xl + k),
        y_down=(c, 4 * y_down + 2 * xl + k),
    )


def meet(peers):
    barrier = pltpu.get_barrier_semaphore()
    for peer in peers:
        pl.semaphore_signal(barrier, inc=1, device_id=peer, device_id_type=MESH)
    pl.semaphore_wait(barrier, len(peers))


class Flows:
    def __init__(self, send_sem, recv_sem):
        self.send_sem, self.recv_sem, self.made = send_sem, recv_sem, []

    def send(self, src, dst, peer):
        n = len(self.made)
        copy = pltpu.make_async_remote_copy(
            src_ref=src,
            dst_ref=dst,
            send_sem=self.send_sem.at[n],
            recv_sem=self.recv_sem.at[n],
            device_id=peer,
            device_id_type=MESH,
        )
        copy.start()
        self.made.append(copy)
        return copy

    def finish(self):
        for copy in self.made:
            copy.wait_send()


GATHER_FLOWS = 40


def gather_kernel(
    keys, values, grad, w, kv, w_all, datt, grad_twin, w_buf, total, send_sem, recv_sem, here_sem
):
    c, f, z, xh, y, xl, k = mesh_spot()
    at = neighbours()
    z_up, z_down, z_far = lax.rem(z + 1, 4), lax.rem(z + 3, 4), lax.rem(z + 2, 4)
    y_up, y_down, y_far = lax.rem(y + 1, 4), lax.rem(y + 3, 4), lax.rem(y + 2, 4)
    rows = keys.shape[0]
    half = w.shape[0] // 2
    meet(list(at.values()))
    flows = Flows(send_sem, recv_sem)

    def chunk(a, who):
        return kv.at[a, pl.ds(pl.multiple_of(who * rows, rows), rows), :]

    def shard(yy, xx, kk):
        return 4 * yy + 2 * xx + kk

    def whole(who):
        return w_buf.at[who]

    def part(who, p):
        return w_buf.at[who, pl.ds(p * half, half), :]

    own = (keys, values)
    kv_far = [flows.send(own[a], chunk(a, c), at["far"]) for a in (0, 1)]
    kv_up = [flows.send(own[a], chunk(a, c), at["z_up"]) for a in (0, 1)]
    kv_down = [flows.send(own[a], chunk(a, c), at["z_down"]) for a in (1, 0)][::-1]
    w_up = flows.send(w, whole(f), at["y_up"])
    w_down = flows.send(w, whole(f), at["y_down"])
    w_side = [
        flows.send(w.at[pl.ds(p * half, half), :], part(f, p), at[("near", "back")[p]])
        for p in (0, 1)
    ]
    to_twin = [flows.send(w, whole(f), at["twin"])]
    swap = flows.send(grad, grad_twin, at["twin"])
    here = [
        pltpu.make_async_copy(keys, chunk(0, c), here_sem.at[0]),
        pltpu.make_async_copy(values, chunk(1, c), here_sem.at[1]),
        pltpu.make_async_copy(w, whole(f), here_sem.at[2]),
    ]
    for copy in here:
        copy.start()

    kv_up[0].wait_recv()
    on_k = flows.send(chunk(0, 2 * z_down + xh), chunk(0, 2 * z_down + xh), at["z_up"])
    kv_down[1].wait_recv()
    on_v = flows.send(chunk(1, 2 * z_up + xh), chunk(1, 2 * z_up + xh), at["z_down"])
    w_up.wait_recv()
    got = shard(y_down, xl, k)
    on_w0 = flows.send(part(got, 0), part(got, 0), at["y_up"])
    to_twin.append(flows.send(whole(got), whole(got), at["twin"]))
    w_down.wait_recv()
    got = shard(y_up, xl, k)
    on_w1 = flows.send(part(got, 1), part(got, 1), at["y_down"])
    to_twin.append(flows.send(whole(got), whole(got), at["twin"]))

    other = 2 * z + 1 - xh
    side = shard(y, 1 - xl, k)
    pair_up, pair_down = [None, None], [None, None]
    for a in (0, 1):
        kv_far[a].wait_recv()
        pair_up[a] = flows.send(chunk(a, other), chunk(a, other), at["z_up"])
        pair_down[a] = flows.send(chunk(a, other), chunk(a, other), at["z_down"])
    side_up, side_down = [], []
    for p in (0, 1):
        w_side[p].wait_recv()
        side_up.append(flows.send(part(side, p), part(side, p), at["y_up"]))
        side_down.append(flows.send(part(side, p), part(side, p), at["y_down"]))
    to_twin.append(flows.send(whole(side), whole(side), at["twin"]))

    def multiply(yy, first):
        def columns(n, carry):
            lanes = pl.ds(pl.multiple_of(n * 512, 512), 512)
            out = None
            for s in range(4):
                who = 4 * yy + s
                g = grad[:, pl.ds(pl.multiple_of(who * HEAD_DIM, HEAD_DIM), HEAD_DIM)]
                term = dot(g, w_buf[who, lanes, :], 1, 1)
                out = term if out is None else out + term
            total[:, lanes] = out if first else total[:, lanes] + out
            return carry

        lax.fori_loop(0, total.shape[1] // 512, columns, 0)

    kv_up[1].wait_recv()
    kv_down[0].wait_recv()
    got = shard(y_down, 1 - xl, k)
    side_up[0].wait_recv()
    on_s0 = flows.send(part(got, 0), part(got, 0), at["y_up"])
    side_up[1].wait_recv()
    to_twin.append(flows.send(whole(got), whole(got), at["twin"]))
    got = shard(y_up, 1 - xl, k)
    side_down[0].wait_recv()
    side_down[1].wait_recv()
    on_s1 = flows.send(part(got, 1), part(got, 1), at["y_down"])
    to_twin.append(flows.send(whole(got), whole(got), at["twin"]))

    pair_up[0].wait_recv()
    got = 2 * z_down + 1 - xh
    pair_on_k = flows.send(chunk(0, got), chunk(0, got), at["z_up"])
    pair_down[1].wait_recv()
    got = 2 * z_up + 1 - xh
    pair_on_v = flows.send(chunk(1, got), chunk(1, got), at["z_down"])

    got = shard(y_far, xl, k)
    on_w0.wait_recv()
    to_twin.append(flows.send(part(got, 0), part(got, 0), at["twin"]))
    on_w1.wait_recv()
    to_twin.append(flows.send(part(got, 1), part(got, 1), at["twin"]))
    for copy in here:
        copy.wait()
    for n in (0, 3):
        to_twin[n].wait_recv()
    multiply(y, True)
    for n in (1, 4):
        to_twin[n].wait_recv()
    multiply(y_down, False)
    for n in (2, 5):
        to_twin[n].wait_recv()
    multiply(y_up, False)

    got = shard(y_far, 1 - xl, k)
    on_s0.wait_recv()
    to_twin.append(flows.send(part(got, 0), part(got, 0), at["twin"]))
    on_s1.wait_recv()
    to_twin.append(flows.send(part(got, 1), part(got, 1), at["twin"]))
    for n in (6, 7, 8, 9):
        to_twin[n].wait_recv()
    multiply(y_far, False)
    out = pltpu.make_async_copy(w_buf, w_all, here_sem.at[3])
    out.start()
    datt[...] = total[...].astype(BF16)
    swap.wait_recv()
    on_k.wait_recv()
    on_v.wait_recv()
    pair_up[1].wait_recv()
    pair_down[0].wait_recv()
    pair_on_k.wait_recv()
    pair_on_v.wait_recv()
    flows.finish()
    out.wait()


def gather(keys, values, grad, w):
    rows, kv_cols = keys.shape
    feats, cols = w.shape
    n_ctx, n_fsdp = lax.axis_size("ctx"), lax.axis_size("fsdp")
    hbm = pl.BlockSpec(memory_space=pltpu.HBM)
    vmem = pl.BlockSpec(memory_space=pltpu.VMEM)
    return pl.pallas_call(
        gather_kernel,
        in_specs=[hbm, hbm, vmem, hbm],
        out_specs=[hbm, hbm, vmem, hbm],
        out_shape=[
            jax.ShapeDtypeStruct((2, n_ctx * rows, kv_cols), BF16),
            jax.ShapeDtypeStruct((n_fsdp, feats, cols), BF16),
            jax.ShapeDtypeStruct((rows, feats), BF16),
            jax.ShapeDtypeStruct(grad.shape, BF16),
        ],
        scratch_shapes=[
            pltpu.VMEM((n_fsdp, feats, cols), BF16),
            pltpu.VMEM((rows, feats), F32),
            pltpu.SemaphoreType.DMA((GATHER_FLOWS,)),
            pltpu.SemaphoreType.DMA((GATHER_FLOWS,)),
            pltpu.SemaphoreType.DMA((4,)),
        ],
        compiler_params=pltpu.CompilerParams(
            collective_id=0, has_side_effects=True, vmem_limit_bytes=40 << 20
        ),
        cost_estimate=pl.CostEstimate(
            flops=2 * rows * feats * feats, bytes_accessed=24 << 20, transcendentals=0
        ),
        name="gather",
    )(keys, values, grad, w)


REDUCE_FLOWS = 41
PIECES = 2


def reduce_kernel(
    dk, dv, att, att_t, grad, grad_twin, resid, w_all,
    mixed, dk_out, dv_out, proj,
    att_twin, w_buf, att_buf, res_buf, ahead, mine, hop_in, raw_in, sum_in, sum_out, kept, far_out, far_in,
    far_p, up_keep, down_keep, own_keep, up_raw, down_raw, top_in, low_in, top_out, low_out,
    top_raw, low_raw, top_sum, low_sum, x_out, x_in, x_keep, z_out, z_in, z_keep,
    send_sem, recv_sem, here_sem,
):
    c, f, z, xh, y, xl, k = mesh_spot()
    at = neighbours()
    z_up, z_down, z_far = lax.rem(z + 1, 4), lax.rem(z + 3, 4), lax.rem(z + 2, 4)
    y_up, y_down, y_far = lax.rem(y + 1, 4), lax.rem(y + 3, 4), lax.rem(y + 2, 4)
    at["z_far"] = (2 * z_far + xh, f)
    rows, kv_cols = dk_out.shape
    pair = 2 * rows
    wide = kv_cols // PIECES
    meet(list(at.values()))
    flows = Flows(send_sem, recv_sem)
    parts = (dk, dv)

    def block(a, zz, p):
        return parts[a].at[
            pl.ds(pl.multiple_of(zz * pair, pair), pair), pl.ds(p * wide, wide)
        ]

    swap = flows.send(att_t, att_twin, at["twin"])
    hops = [
        [
            flows.send(block(0, z_far, p), hop_in.at[0, p], at["z_up"]),
            flows.send(block(1, z_far, p), hop_in.at[1, p], at["z_down"]),
        ]
        for p in range(PIECES)
    ]
    here = []
    for n, (src, dst) in enumerate(
        [
            (dk.at[pl.ds(pl.multiple_of(z_up * pair, pair), pair), :], ahead.at[0]),
            (dv.at[pl.ds(pl.multiple_of(z_down * pair, pair), pair), :], ahead.at[1]),
            (dk.at[pl.ds(pl.multiple_of(z * pair, pair), pair), :], mine.at[0]),
            (dv.at[pl.ds(pl.multiple_of(z * pair, pair), pair), :], mine.at[1]),
            (w_all, w_buf),
            (att, att_buf),
            (resid, res_buf),
        ]
    ):
        copy = pltpu.make_async_copy(src, dst, here_sem.at[n])
        copy.start()
        here.append(copy)

    def product(yy, p, low, store):
        lanes = [
            pl.ds(pl.multiple_of((4 * yy + 2 * s + k) * HEAD_DIM, HEAD_DIM), HEAD_DIM)
            for s in (0, 1)
        ]
        g_own = jnp.concatenate([grad[:, s] for s in lanes], axis=1)
        g_twin = jnp.concatenate([grad_twin[:, s] for s in lanes], axis=1)

        def one(m, carry):
            head = 2 * (m + low) + p
            store(m, dot(att_t[head], g_own, 1, 0) + dot(att_twin[head], g_twin, 1, 0))
            return carry

        lax.fori_loop(0, 4, one, 0)

    def put(ref, p, low=0):
        def store(m, value):
            ref[p, m + low] = value.astype(ref.dtype)

        return store

    swap.wait_recv()
    top_hop, low_hop = [], []
    for p in range(PIECES):
        product(y_far, p, 0, put(far_p, p))
        top_hop.append(flows.send(far_p.at[p, pl.ds(0, 4)], top_in.at[p], at["y_up"]))
        product(y_far, p, 4, put(far_p, p, 4))
        low_hop.append(flows.send(far_p.at[p, pl.ds(4, 4)], low_in.at[p], at["y_down"]))
    raws = [
        [
            flows.send(block(0, z_down, p), raw_in.at[0, p], at["z_down"]),
            flows.send(block(1, z_up, p), raw_in.at[1, p], at["z_up"]),
        ]
        for p in range(PIECES)
    ]
    raw_top, raw_low = [], []
    for p in range(PIECES):
        product(y_up, p, 4, put(up_raw, p))
        raw_low.append(flows.send(up_raw.at[p], low_raw.at[p], at["y_up"]))
        product(y_down, p, 0, put(down_raw, p))
        raw_top.append(flows.send(down_raw.at[p], top_raw.at[p], at["y_down"]))
        product(y_up, p, 0, put(up_keep, p))
        product(y_down, p, 4, put(down_keep, p))

    for copy in here[:4]:
        copy.wait()
    sums = [[None, None] for _ in range(PIECES)]
    top_on, low_on = [], []
    for p in range(PIECES):
        cols = slice(p * wide, (p + 1) * wide)
        for a, towards in ((0, "z_up"), (1, "z_down")):
            hops[p][a].wait_recv()
            sum_out[a, p] = (ahead[a, :, cols].astype(F32) + hop_in[a, p].astype(F32)).astype(BF16)
            sums[p][a] = flows.send(sum_out.at[a, p], sum_in.at[a, p], at[towards])
        top_hop[p].wait_recv()
        top_out[p] = (up_keep[p] + top_in[p].astype(F32)).astype(BF16)
        top_on.append(flows.send(top_out.at[p], top_sum.at[p], at["y_up"]))
        low_hop[p].wait_recv()
        low_out[p] = (down_keep[p] + low_in[p].astype(F32)).astype(BF16)
        low_on.append(flows.send(low_out.at[p], low_sum.at[p], at["y_down"]))
    for p in range(PIECES):
        product(y, p, 0, put(own_keep, p))
        product(y, p, 4, put(own_keep, p, 4))

    for copy in here[4:]:
        copy.wait()

    def project(n, carry):
        lanes = pl.ds(pl.multiple_of(n * HEAD_DIM, HEAD_DIM), HEAD_DIM)
        out = dot(att_buf[...], w_buf[n], 1, 0)
        mixed[:, lanes] = (res_buf[:, lanes].astype(F32) + out).astype(BF16)
        return carry

    lax.fori_loop(0, w_buf.shape[0], project, 0)

    keep_rows = pl.ds(pl.multiple_of(xh * rows, rows), rows)
    give_rows = pl.ds(pl.multiple_of((1 - xh) * rows, rows), rows)
    fars = [[None, None] for _ in range(PIECES)]
    x_to = ("near", "far", "back")
    x_flow = []
    for p in range(PIECES):
        cols = pl.ds(p * wide, wide)
        for a in (0, 1):
            raws[p][a].wait_recv()
            sums[p][a].wait_recv()

            def gathered(which):
                return (
                    mine[a, which, cols].astype(F32)
                    + raw_in[a, p, which, :].astype(F32)
                    + sum_in[a, p, which, :].astype(F32)
                )

            far_out[a, p] = gathered(give_rows).astype(BF16)
            fars[p][a] = flows.send(far_out.at[a, p], far_in.at[a, p], at["far"])
            kept[a, p] = gathered(keep_rows)

        raw_top[p].wait_recv()
        top_on[p].wait_recv()
        raw_low[p].wait_recv()
        low_on[p].wait_recv()
        for m in range(4):
            own_keep[p, m] += top_raw[p, m].astype(F32) + top_sum[p, m].astype(F32)
            own_keep[p, m + 4] += low_raw[p, m].astype(F32) + low_sum[p, m].astype(F32)
        near_lanes = pl.ds(pl.multiple_of((1 - xl) * HEAD_DIM, HEAD_DIM), HEAD_DIM)
        own_lanes = pl.ds(pl.multiple_of(xl * HEAD_DIM, HEAD_DIM), HEAD_DIM)
        sent = []
        for n, (hi, lanes) in enumerate(
            ((xh, near_lanes), (1 - xh, own_lanes), (1 - xh, near_lanes))
        ):
            for zz in range(4):
                x_out[p, n, zz] = own_keep[p, 2 * zz + hi, :, lanes].astype(BF16)
            sent.append(flows.send(x_out.at[p, n], x_in.at[p, n], at[x_to[n]]))
        x_flow.append(sent)
        for zz in range(4):
            x_keep[p, zz] = own_keep[p, 2 * zz + xh, :, own_lanes]

    z_to = (("z_up", z_up), ("z_down", z_down), ("z_far", z_far))
    z_flow = []
    for p in range(PIECES):
        cols = slice(p * wide, (p + 1) * wide)
        for a, out in ((0, dk_out), (1, dv_out)):
            fars[p][a].wait_recv()
            out[:, cols] = (kept[a, p] + far_in[a, p].astype(F32)).astype(BF16)
        for n in range(3):
            x_flow[p][n].wait_recv()
        for zz in range(4):
            total = x_keep[p, zz]
            for n in range(3):
                total += x_in[p, n, zz].astype(F32)
            x_keep[p, zz] = total
        sent = []
        for n, (name, zz) in enumerate(z_to):
            z_out[p, n] = x_keep[p, zz].astype(BF16)
            sent.append(flows.send(z_out.at[p, n], z_in.at[p, n], at[name]))
        z_flow.append(sent)
        z_keep[p] = x_keep[p, z]
    for p in range(PIECES):
        total = z_keep[p]
        for n in range(3):
            z_flow[p][n].wait_recv()
            total += z_in[p, n].astype(F32)
        proj[pl.ds(p * HEAD_DIM, HEAD_DIM), :] = total
    flows.finish()


def reduce(dk, dv, att, att_t, grad, grad_twin, resid, w_all):
    n_ctx = lax.axis_size("ctx")
    seq, kv_cols = dk.shape
    rows, feats = att.shape
    chunk = seq // n_ctx
    heads = att_t.shape[0]
    per = heads // n_ctx
    wide = kv_cols // PIECES
    hbm = pl.BlockSpec(memory_space=pltpu.HBM)
    vmem = pl.BlockSpec(memory_space=pltpu.VMEM)

    def quad(dtype, n=4, lanes=2 * HEAD_DIM):
        return pltpu.VMEM((PIECES, n, HEAD_DIM, lanes), dtype)

    def kv_buf(height, dtype=BF16):
        return pltpu.VMEM((2, PIECES, height, wide), dtype)

    return pl.pallas_call(
        reduce_kernel,
        in_specs=[hbm, hbm, hbm, vmem, vmem, vmem, hbm, hbm],
        out_specs=[vmem] * 4,
        out_shape=[
            jax.ShapeDtypeStruct((rows, feats), BF16),
            jax.ShapeDtypeStruct((chunk, kv_cols), BF16),
            jax.ShapeDtypeStruct((chunk, kv_cols), BF16),
            jax.ShapeDtypeStruct((per * HEAD_DIM, HEAD_DIM), F32),
        ],
        scratch_shapes=[
            pltpu.VMEM(att_t.shape, BF16),
            pltpu.VMEM(w_all.shape, BF16),
            pltpu.VMEM(att.shape, BF16),
            pltpu.VMEM(resid.shape, BF16),
            pltpu.VMEM((2, 2 * chunk, kv_cols), BF16),
            pltpu.VMEM((2, 2 * chunk, kv_cols), BF16),
            kv_buf(2 * chunk),
            kv_buf(2 * chunk),
            kv_buf(2 * chunk),
            kv_buf(2 * chunk),
            kv_buf(chunk, F32),
            kv_buf(chunk),
            kv_buf(chunk),
            quad(BF16, 8),
            quad(F32),
            quad(F32),
            quad(F32, 8),
            quad(BF16),
            quad(BF16),
            quad(BF16),
            quad(BF16),
            quad(BF16),
            quad(BF16),
            quad(BF16),
            quad(BF16),
            quad(BF16),
            quad(BF16),
            pltpu.VMEM((PIECES, 3, 4, HEAD_DIM, HEAD_DIM), BF16),
            pltpu.VMEM((PIECES, 3, 4, HEAD_DIM, HEAD_DIM), BF16),
            quad(F32, 4, HEAD_DIM),
            quad(BF16, 3, HEAD_DIM),
            quad(BF16, 3, HEAD_DIM),
            pltpu.VMEM((PIECES, HEAD_DIM, HEAD_DIM), F32),
            pltpu.SemaphoreType.DMA((REDUCE_FLOWS,)),
            pltpu.SemaphoreType.DMA((REDUCE_FLOWS,)),
            pltpu.SemaphoreType.DMA((7,)),
        ],
        compiler_params=pltpu.CompilerParams(
            collective_id=1, has_side_effects=True, vmem_limit_bytes=52 << 20
        ),
        cost_estimate=pl.CostEstimate(
            flops=4 * rows * feats * feats, bytes_accessed=24 << 20, transcendentals=0
        ),
        name="reduce",
    )(dk, dv, att, att_t, grad, grad_twin, resid, w_all)


def local(queries, keys, values, resid, grad_out, w_out, block_list, block_count):
    grad = grad_out[0]
    kv, w_all, datt, grad_twin = gather(keys[0], values[0], grad, w_out)
    att, att_t, dq, dk, dv = attention(queries[0], datt, kv, block_list, block_count)
    mixed, dk, dv, proj = reduce(dk, dv, att, att_t, grad, grad_twin, resid[0], w_all)
    return mixed[None], dq[None], dk[None], dv[None], proj


def solution(mesh):
    rows = P("fsdp", "ctx", None)
    in_specs = (rows, rows, rows, rows, rows, P(None, "fsdp"), P("ctx", None), P("ctx"))
    out_specs = (rows, rows, rows, rows, P("ctx", "fsdp"))
    return jax.shard_map(local, mesh=mesh, in_specs=in_specs, out_specs=out_specs, check_vma=False)
```

```python
import functools
import itertools
import math

import jax
import jax.numpy as jnp
from jax import lax
from jax.experimental import pallas as pl
from jax.experimental.pallas import tpu as pltpu
from jax.sharding import PartitionSpec as P

QUERY_HEADS = 16
KV_HEADS = 4
GROUP = QUERY_HEADS // KV_HEADS
HEAD_DIM = 128
BLOCK = 128
SLOTS = 8
STEP = 4
SCALE = 1.0 / math.sqrt(HEAD_DIM)
BF16 = jnp.bfloat16
F32 = jnp.float32
LOG2E = math.log2(math.e)
MESH = pl.DeviceIdType.MESH


def dot(a, b, ca, cb):
    return lax.dot_general(a, b, (((ca,), (cb,)), ((), ())), preferred_element_type=F32)


def stack_heads(ref, i):
    rows = slice(i * BLOCK, (i + 1) * BLOCK)
    return jnp.concatenate(
        [ref[rows, h * HEAD_DIM : (h + 1) * HEAD_DIM] for h in range(GROUP)], axis=0
    )


def attention_kernel(
    list_ref, count_ref, q_ref, do_ref, k_ref, v_ref,
    att_ref, att_t_ref, dq_ref, dk_ref, dv_ref, dk_acc, dv_acc,
):
    cols = GROUP * BLOCK
    count = q_ref.shape[0] // BLOCK
    dk_acc[...] = jnp.zeros_like(dk_acc)
    dv_acc[...] = jnp.zeros_like(dv_acc)

    def slots(ns):
        key_pos = lax.broadcasted_iota(jnp.int32, (BLOCK, cols), 0)
        query_pos = lax.broadcasted_iota(jnp.int32, (BLOCK, cols), 1) % BLOCK
        rows, k_sel, v_sel, qs, dos = [], [], [], [], []
        for i, n in enumerate(ns):
            rows.append(
                [pl.ds(pl.multiple_of(list_ref[i, j] * BLOCK, BLOCK), BLOCK) for j in range(n)]
            )
            k_sel.append(jnp.concatenate([k_ref[0, r, :] for r in rows[i]], axis=0))
            v_sel.append(jnp.concatenate([v_ref[0, r, :] for r in rows[i]], axis=0))
            qs.append(stack_heads(q_ref, i))
            dos.append(stack_heads(do_ref, i))
        scores = [dot(k, q, 1, 1) for k, q in zip(k_sel, qs)]
        prob_grads = [dot(v, do, 1, 1) for v, do in zip(v_sel, dos)]
        probs, rounded = [], []
        for i, (s, n) in enumerate(zip(scores, ns)):
            parts = [jnp.where(key_pos <= query_pos, s[:BLOCK], -1e30)]
            if n > STEP:
                parts.append(s[BLOCK : (n - STEP + 1) * BLOCK])
            for j in range(n - STEP + 1, n):
                dead = jnp.where(j < count_ref[i], 0.0, -1e30).astype(F32)
                parts.append(s[j * BLOCK : (j + 1) * BLOCK] + dead)
            s = jnp.concatenate(parts, axis=0)
            top = jnp.max(s, axis=0, keepdims=True)
            e = jnp.exp2((s - top) * (SCALE * LOG2E))
            p = e * (1.0 / jnp.sum(e, axis=0, keepdims=True))
            probs.append(p)
            rounded.append(p.astype(BF16))
        outs = [dot(v, pb, 0, 0).astype(BF16) for v, pb in zip(v_sel, rounded)]
        row_dots = [
            jnp.sum(o.astype(F32) * do.T.astype(F32), axis=0, keepdims=True)
            for o, do in zip(outs, dos)
        ]
        grads = [
            (p * (dp - r)).astype(BF16) for p, dp, r in zip(probs, prob_grads, row_dots)
        ]
        dqs = [(dot(k, ds, 0, 0) * SCALE).astype(BF16).T for k, ds in zip(k_sel, grads)]
        dks = [dot(ds, q, 1, 0) for ds, q in zip(grads, qs)]
        dvs = [dot(pb, do, 1, 0) for pb, do in zip(rounded, dos)]
        for i, (o_t, dq) in enumerate(zip(outs, dqs)):
            o = o_t.T
            mine = slice(i * BLOCK, (i + 1) * BLOCK)
            for h in range(GROUP):
                lanes = slice(h * HEAD_DIM, (h + 1) * HEAD_DIM)
                here = slice(h * BLOCK, (h + 1) * BLOCK)
                att_ref[mine, lanes] = o[here]
                dq_ref[mine, lanes] = dq[here]
                att_t_ref[h, :, mine] = o_t[:, here]
        for i, n in enumerate(ns):
            for j in range(n):
                here = slice(j * BLOCK, (j + 1) * BLOCK)
                dk_acc[rows[i][j], :] += dks[i][here]
                dv_acc[rows[i][j], :] += dvs[i][here]

    need = [(count_ref[i] + STEP - 1) // STEP for i in range(count)]
    for ns in itertools.product(range(STEP, SLOTS + 1, STEP), repeat=count):
        hit = functools.reduce(
            jnp.logical_and, [have == n // STEP for have, n in zip(need, ns)]
        )
        pl.when(hit)(functools.partial(slots, ns))

    dk_ref[...] = (dk_acc[...] * SCALE).astype(BF16)
    dv_ref[...] = dv_acc[...].astype(BF16)


def attention(queries, datt, kv, block_list, block_count):
    rows, width = queries.shape
    seq = kv.shape[1]
    group_cols = GROUP * HEAD_DIM
    kv_cols = KV_HEADS * HEAD_DIM
    q_spec = pl.BlockSpec((rows, group_cols), lambda g, *_: (0, g))

    def kv_spec(which):
        return pl.BlockSpec((1, seq, HEAD_DIM), lambda g, *_: (which, 0, g))

    out_spec = pl.BlockSpec((seq, HEAD_DIM), lambda g, *_: (0, g))
    t_spec = pl.BlockSpec((GROUP, HEAD_DIM, rows), lambda g, *_: (g, 0, 0))
    flops = 12 * rows * QUERY_HEADS * SLOTS * BLOCK * HEAD_DIM
    return pl.pallas_call(
        attention_kernel,
        grid_spec=pltpu.PrefetchScalarGridSpec(
            num_scalar_prefetch=2,
            grid=(KV_HEADS,),
            in_specs=[q_spec, q_spec, kv_spec(0), kv_spec(1)],
            out_specs=[q_spec, t_spec, q_spec, out_spec, out_spec],
            scratch_shapes=[pltpu.VMEM((seq, HEAD_DIM), F32)] * 2,
        ),
        out_shape=[
            jax.ShapeDtypeStruct((rows, width), BF16),
            jax.ShapeDtypeStruct((QUERY_HEADS, HEAD_DIM, rows), BF16),
            jax.ShapeDtypeStruct((rows, width), BF16),
            jax.ShapeDtypeStruct((seq, kv_cols), BF16),
            jax.ShapeDtypeStruct((seq, kv_cols), BF16),
        ],
        compiler_params=pltpu.CompilerParams(
            dimension_semantics=("arbitrary",), vmem_limit_bytes=60 << 20
        ),
        cost_estimate=pl.CostEstimate(
            flops=flops, bytes_accessed=12 << 20, transcendentals=rows * QUERY_HEADS * SLOTS * BLOCK
        ),
        name="attention",
    )(block_list, block_count, queries, datt, kv, kv)


def mesh_spot():
    c, f = lax.axis_index("ctx"), lax.axis_index("fsdp")
    return c, f, c // 2, lax.rem(c, 2), f // 4, lax.rem(f // 2, 2), lax.rem(f, 2)


def neighbours():
    c, f, z, xh, y, xl, k = mesh_spot()
    z_up, z_down = lax.rem(z + 1, 4), lax.rem(z + 3, 4)
    y_up, y_down = lax.rem(y + 1, 4), lax.rem(y + 3, 4)
    side, far, twin = 4 * y + 2 * (1 - xl) + k, 2 * z + 1 - xh, 4 * y + 2 * xl + 1 - k
    return dict(
        far=(far, f),
        near=(c, side),
        back=(far, side),
        twin=(c, twin),
        z_up=(2 * z_up + xh, f),
        z_down=(2 * z_down + xh, f),
        y_up=(c, 4 * y_up + 2 * xl + k),
        y_down=(c, 4 * y_down + 2 * xl + k),
    )


def meet(peers):
    barrier = pltpu.get_barrier_semaphore()
    for peer in peers:
        pl.semaphore_signal(barrier, inc=1, device_id=peer, device_id_type=MESH)
    pl.semaphore_wait(barrier, len(peers))


class Flows:
    def __init__(self, send_sem, recv_sem):
        self.send_sem, self.recv_sem, self.made = send_sem, recv_sem, []

    def send(self, src, dst, peer):
        n = len(self.made)
        copy = pltpu.make_async_remote_copy(
            src_ref=src,
            dst_ref=dst,
            send_sem=self.send_sem.at[n],
            recv_sem=self.recv_sem.at[n],
            device_id=peer,
            device_id_type=MESH,
        )
        copy.start()
        self.made.append(copy)
        return copy

    def finish(self):
        for copy in self.made:
            copy.wait_send()


GATHER_FLOWS = 40


def gather_kernel(
    keys, values, grad, w, kv, w_all, datt, grad_twin, w_buf, total, send_sem, recv_sem, here_sem
):
    c, f, z, xh, y, xl, k = mesh_spot()
    at = neighbours()
    z_up, z_down, z_far = lax.rem(z + 1, 4), lax.rem(z + 3, 4), lax.rem(z + 2, 4)
    y_up, y_down, y_far = lax.rem(y + 1, 4), lax.rem(y + 3, 4), lax.rem(y + 2, 4)
    rows = keys.shape[0]
    half = w.shape[0] // 2
    meet(list(at.values()))
    flows = Flows(send_sem, recv_sem)

    def chunk(a, who):
        return kv.at[a, pl.ds(pl.multiple_of(who * rows, rows), rows), :]

    def shard(yy, xx, kk):
        return 4 * yy + 2 * xx + kk

    def whole(who):
        return w_buf.at[who]

    def part(who, p):
        return w_buf.at[who, pl.ds(p * half, half), :]

    own = (keys, values)
    w_side = [
        flows.send(w.at[pl.ds(p * half, half), :], part(f, p), at[("near", "back")[p]])
        for p in (0, 1)
    ]
    w_up = flows.send(w, whole(f), at["y_up"])
    w_down = flows.send(w, whole(f), at["y_down"])
    kv_up = [flows.send(own[a], chunk(a, c), at["z_up"]) for a in (0, 1)]
    kv_down = [flows.send(own[a], chunk(a, c), at["z_down"]) for a in (1, 0)][::-1]
    kv_far = [flows.send(own[a], chunk(a, c), at["far"]) for a in (0, 1)]
    to_twin = [flows.send(w, whole(f), at["twin"])]
    swap = flows.send(grad, grad_twin, at["twin"])
    here = [
        pltpu.make_async_copy(keys, chunk(0, c), here_sem.at[0]),
        pltpu.make_async_copy(values, chunk(1, c), here_sem.at[1]),
        pltpu.make_async_copy(w, whole(f), here_sem.at[2]),
    ]
    for copy in here:
        copy.start()

    side = shard(y, 1 - xl, k)
    side_up, side_down = [], []

    def pass_side(p):
        w_side[p].wait_recv()
        side_up.append(flows.send(part(side, p), part(side, p), at["y_up"]))
        side_down.append(flows.send(part(side, p), part(side, p), at["y_down"]))

    pass_side(0)
    kv_up[0].wait_recv()
    got_k = 2 * z_down + xh
    on_k = flows.send(chunk(0, got_k), chunk(0, got_k), at["z_up"])
    kv_down[1].wait_recv()
    got_v = 2 * z_up + xh
    on_v = flows.send(chunk(1, got_v), chunk(1, got_v), at["z_down"])
    w_up.wait_recv()
    got = shard(y_down, xl, k)
    on_w0 = flows.send(part(got, 0), part(got, 0), at["y_up"])
    to_twin.append(flows.send(whole(got), whole(got), at["twin"]))
    w_down.wait_recv()
    got = shard(y_up, xl, k)
    on_w1 = flows.send(part(got, 1), part(got, 1), at["y_down"])
    to_twin.append(flows.send(whole(got), whole(got), at["twin"]))
    pass_side(1)
    to_twin.append(flows.send(whole(side), whole(side), at["twin"]))

    other = 2 * z + 1 - xh
    pair_up, pair_down = [None, None], [None, None]
    for a in (0, 1):
        kv_far[a].wait_recv()
        pair_up[a] = flows.send(chunk(a, other), chunk(a, other), at["z_up"])
        pair_down[a] = flows.send(chunk(a, other), chunk(a, other), at["z_down"])

    def multiply(yy, n):
        slab = pl.ds(pl.multiple_of(4 * yy, 4), 4)
        out = pltpu.make_async_copy(w_buf.at[slab], w_all.at[slab], here_sem.at[3 + n])
        out.start()
        here.append(out)

        def columns(b, carry):
            lanes = pl.ds(pl.multiple_of(b * 512, 512), 512)
            out = None
            for s in range(4):
                who = 4 * yy + s
                g = grad[:, pl.ds(pl.multiple_of(who * HEAD_DIM, HEAD_DIM), HEAD_DIM)]
                term = dot(g, w_buf[who, lanes, :], 1, 1)
                out = term if out is None else out + term
            total[:, lanes] = out if n == 0 else total[:, lanes] + out
            return carry

        lax.fori_loop(0, total.shape[1] // 512, columns, 0)

    here.pop().wait()
    for n in (0, 3):
        to_twin[n].wait_recv()
    multiply(y, 0)

    def piece(a, who, p):
        start = pl.multiple_of(who * rows, rows) + p * (rows // 2)
        return kv.at[a, pl.ds(start, rows // 2), :]

    on_k.wait_recv()
    got = 2 * z_far + xh
    cross_k = flows.send(piece(0, got, 1), piece(0, got, 1), at["far"])
    on_v.wait_recv()
    cross_v = flows.send(piece(1, got, 1), piece(1, got, 1), at["far"])
    got = shard(y_far, xl, k)
    on_w0.wait_recv()
    on_s0 = flows.send(part(got, 0), part(got, 0), at["near"])
    to_twin.append(flows.send(part(got, 0), part(got, 0), at["twin"]))
    on_w1.wait_recv()
    on_s1 = flows.send(part(got, 1), part(got, 1), at["back"])
    to_twin.append(flows.send(part(got, 1), part(got, 1), at["twin"]))

    pair_up[0].wait_recv()
    got = 2 * z_down + 1 - xh
    pair_on_k = flows.send(piece(0, got, 0), piece(0, got, 0), at["z_up"])
    pair_down[1].wait_recv()
    got = 2 * z_up + 1 - xh
    pair_on_v = flows.send(piece(1, got, 0), piece(1, got, 0), at["z_down"])

    for yy, arrived in ((y_down, side_up), (y_up, side_down)):
        got = shard(yy, 1 - xl, k)
        for copy in arrived:
            copy.wait_recv()
        to_twin.append(flows.send(whole(got), whole(got), at["twin"]))
    got = shard(y_far, 1 - xl, k)
    on_s0.wait_recv()
    to_twin.append(flows.send(part(got, 0), part(got, 0), at["twin"]))
    on_s1.wait_recv()
    to_twin.append(flows.send(part(got, 1), part(got, 1), at["twin"]))
    for n in (1, 6):
        to_twin[n].wait_recv()
    multiply(y_down, 1)
    for n in (2, 7):
        to_twin[n].wait_recv()
    multiply(y_up, 2)
    for n in (4, 5, 8, 9):
        to_twin[n].wait_recv()
    multiply(y_far, 3)
    datt[...] = total[...].astype(BF16)
    for copy in (swap, kv_up[1], kv_down[0], pair_up[1], pair_down[0]):
        copy.wait_recv()
    for copy in (cross_k, cross_v, pair_on_k, pair_on_v):
        copy.wait_recv()
    flows.finish()
    for copy in here:
        copy.wait()


def gather(keys, values, grad, w):
    rows, kv_cols = keys.shape
    feats, cols = w.shape
    n_ctx, n_fsdp = lax.axis_size("ctx"), lax.axis_size("fsdp")
    hbm = pl.BlockSpec(memory_space=pltpu.HBM)
    vmem = pl.BlockSpec(memory_space=pltpu.VMEM)
    return pl.pallas_call(
        gather_kernel,
        in_specs=[hbm, hbm, vmem, hbm],
        out_specs=[hbm, hbm, vmem, hbm],
        out_shape=[
            jax.ShapeDtypeStruct((2, n_ctx * rows, kv_cols), BF16),
            jax.ShapeDtypeStruct((n_fsdp, feats, cols), BF16),
            jax.ShapeDtypeStruct((rows, feats), BF16),
            jax.ShapeDtypeStruct(grad.shape, BF16),
        ],
        scratch_shapes=[
            pltpu.VMEM((n_fsdp, feats, cols), BF16),
            pltpu.VMEM((rows, feats), F32),
            pltpu.SemaphoreType.DMA((GATHER_FLOWS,)),
            pltpu.SemaphoreType.DMA((GATHER_FLOWS,)),
            pltpu.SemaphoreType.DMA((7,)),
        ],
        compiler_params=pltpu.CompilerParams(
            collective_id=0, has_side_effects=True, vmem_limit_bytes=60 << 20
        ),
        cost_estimate=pl.CostEstimate(
            flops=2 * rows * feats * feats, bytes_accessed=24 << 20, transcendentals=0
        ),
        name="gather",
    )(keys, values, grad, w)


REDUCE_FLOWS = 66
PIECES = 2
PARTS = 4
PART_ROWS = 2 * HEAD_DIM // PARTS


def reduce_kernel(
    dk, dv, att, att_t, grad, grad_twin, resid, w_all,
    mixed, dk_out, dv_out, proj,
    att_twin, w_buf, att_buf, res_buf, ahead, mine, hop_in, raw_in, sum_in, sum_out, kept, far_out, far_in,
    far_p, own_keep, up_raw, down_raw, top_in, low_in, top_out, low_out,
    top_raw, low_raw, top_sum, low_sum, x_out, x_in, x_keep, z_out, z_in,
    send_sem, recv_sem, here_sem,
):
    c, f, z, xh, y, xl, k = mesh_spot()
    at = neighbours()
    z_up, z_down, z_far = lax.rem(z + 1, 4), lax.rem(z + 3, 4), lax.rem(z + 2, 4)
    y_up, y_down, y_far = lax.rem(y + 1, 4), lax.rem(y + 3, 4), lax.rem(y + 2, 4)
    at["z_far"] = (2 * z_far + xh, f)
    rows, kv_cols = dk_out.shape
    pair = 2 * rows
    wide = kv_cols // PIECES
    meet(list(at.values()))
    flows = Flows(send_sem, recv_sem)
    parts = (dk, dv)

    def block(a, zz, p):
        return parts[a].at[
            pl.ds(pl.multiple_of(zz * pair, pair), pair), pl.ds(p * wide, wide)
        ]

    swap = flows.send(att_t, att_twin, at["twin"])
    hops = [
        [
            flows.send(block(0, z_far, p), hop_in.at[0, p], at["z_up"]),
            flows.send(block(1, z_far, p), hop_in.at[1, p], at["z_down"]),
        ]
        for p in range(PIECES)
    ]
    here = []
    for n, (src, dst) in enumerate(
        [
            (dk.at[pl.ds(pl.multiple_of(z_up * pair, pair), pair), :], ahead.at[0]),
            (dv.at[pl.ds(pl.multiple_of(z_down * pair, pair), pair), :], ahead.at[1]),
            (dk.at[pl.ds(pl.multiple_of(z * pair, pair), pair), :], mine.at[0]),
            (dv.at[pl.ds(pl.multiple_of(z * pair, pair), pair), :], mine.at[1]),
            (w_all, w_buf),
            (att, att_buf),
            (resid, res_buf),
        ]
    ):
        copy = pltpu.make_async_copy(src, dst, here_sem.at[n])
        copy.start()
        here.append(copy)

    def product(yy, p, low):
        lanes = [
            pl.ds(pl.multiple_of((4 * yy + 2 * s + k) * HEAD_DIM, HEAD_DIM), HEAD_DIM)
            for s in (0, 1)
        ]
        first, of = p % (PARTS // 2) * PART_ROWS, p // (PARTS // 2)

        def term(left, right):
            heads = [left[2 * (m + low) + of, first : first + PART_ROWS] for m in range(4)]
            wide = jnp.concatenate([right[:, s] for s in lanes], axis=1)
            return dot(jnp.concatenate(heads, axis=0), wide, 1, 0)

        out = term(att_t, grad) + term(att_twin, grad_twin)
        return out.reshape(4, PART_ROWS, 2 * HEAD_DIM)

    swap.wait_recv()
    top_hop, low_hop = [], []
    for p in range(PARTS):
        far_p[p, 0:4] = product(y_far, p, 0).astype(BF16)
        top_hop.append(flows.send(far_p.at[p, pl.ds(0, 4)], top_in.at[p], at["y_up"]))
        far_p[p, 4:8] = product(y_far, p, 4).astype(BF16)
        low_hop.append(flows.send(far_p.at[p, pl.ds(4, 4)], low_in.at[p], at["y_down"]))
    for copy in here[:4]:
        copy.wait()
    raws, sums = [], []
    raw_top, raw_low, top_on, low_on = [], [], [], []

    def relay_kv(p):
        cols = slice(p * wide, (p + 1) * wide)
        raws.append(
            [
                flows.send(block(0, z_down, p), raw_in.at[0, p], at["z_down"]),
                flows.send(block(1, z_up, p), raw_in.at[1, p], at["z_up"]),
            ]
        )
        sums.append([])
        for a, towards in ((0, "z_up"), (1, "z_down")):
            hops[p][a].wait_recv()
            sum_out[a, p] = (ahead[a, :, cols].astype(F32) + hop_in[a, p].astype(F32)).astype(BF16)
            sums[p].append(flows.send(sum_out.at[a, p], sum_in.at[a, p], at[towards]))

    for p in range(PARTS):
        up_raw[p] = product(y_up, p, 4).astype(BF16)
        raw_low.append(flows.send(up_raw.at[p], low_raw.at[p], at["y_up"]))
        down_raw[p] = product(y_down, p, 0).astype(BF16)
        raw_top.append(flows.send(down_raw.at[p], top_raw.at[p], at["y_down"]))
        keep = product(y_up, p, 0)
        top_hop[p].wait_recv()
        top_out[p] = (keep + top_in[p].astype(F32)).astype(BF16)
        top_on.append(flows.send(top_out.at[p], top_sum.at[p], at["y_up"]))
        keep = product(y_down, p, 4)
        low_hop[p].wait_recv()
        low_out[p] = (keep + low_in[p].astype(F32)).astype(BF16)
        low_on.append(flows.send(low_out.at[p], low_sum.at[p], at["y_down"]))
        if p % 2:
            relay_kv(p // 2)
    for p in range(PARTS):
        own_keep[p, 0:4] = product(y, p, 0)
        own_keep[p, 4:8] = product(y, p, 4)

    for copy in here[4:]:
        copy.wait()

    def project(n, carry):
        lanes = pl.ds(pl.multiple_of(n * HEAD_DIM, HEAD_DIM), HEAD_DIM)
        out = dot(att_buf[...], w_buf[n], 1, 0)
        mixed[:, lanes] = (res_buf[:, lanes].astype(F32) + out).astype(BF16)
        return carry

    def mix(quarter):
        many = w_buf.shape[0] // 4
        lax.fori_loop(quarter * many, (quarter + 1) * many, project, 0)

    keep_rows = pl.ds(pl.multiple_of(xh * rows, rows), rows)
    give_rows = pl.ds(pl.multiple_of((1 - xh) * rows, rows), rows)
    fars, x_flow, z_flow = [], [], []
    x_to = ("near", "far", "back")
    z_to = (("z_up", z_up), ("z_down", z_down), ("z_far", z_far))
    near_lanes = pl.ds(pl.multiple_of((1 - xl) * HEAD_DIM, HEAD_DIM), HEAD_DIM)
    own_lanes = pl.ds(pl.multiple_of(xl * HEAD_DIM, HEAD_DIM), HEAD_DIM)

    def cross_kv(p):
        cols = pl.ds(p * wide, wide)
        fars.append([])
        for a in (0, 1):
            raws[p][a].wait_recv()
            sums[p][a].wait_recv()

            def gathered(which):
                return (
                    mine[a, which, cols].astype(F32)
                    + raw_in[a, p, which, :].astype(F32)
                    + sum_in[a, p, which, :].astype(F32)
                )

            far_out[a, p] = gathered(give_rows).astype(BF16)
            fars[p].append(flows.send(far_out.at[a, p], far_in.at[a, p], at["far"]))
            kept[a, p] = gathered(keep_rows)

    def cross(p):
        raw_top[p].wait_recv()
        top_on[p].wait_recv()
        raw_low[p].wait_recv()
        low_on[p].wait_recv()
        for m in range(4):
            own_keep[p, m] += top_raw[p, m].astype(F32) + top_sum[p, m].astype(F32)
            own_keep[p, m + 4] += low_raw[p, m].astype(F32) + low_sum[p, m].astype(F32)
        sent = []
        for n, (hi, lanes) in enumerate(
            ((xh, near_lanes), (1 - xh, own_lanes), (1 - xh, near_lanes))
        ):
            for zz in range(4):
                x_out[p, n, zz] = own_keep[p, 2 * zz + hi, :, lanes].astype(BF16)
            sent.append(flows.send(x_out.at[p, n], x_in.at[p, n], at[x_to[n]]))
        x_flow.append(sent)

    def along(p):
        for n in range(3):
            x_flow[p][n].wait_recv()
        for zz in range(4):
            total = own_keep[p, 2 * zz + xh, :, own_lanes]
            for n in range(3):
                total += x_in[p, n, zz].astype(F32)
            x_keep[p, zz] = total
        sent = []
        for n, (name, zz) in enumerate(z_to):
            z_out[p, n] = x_keep[p, zz].astype(BF16)
            sent.append(flows.send(z_out.at[p, n], z_in.at[p, n], at[name]))
        z_flow.append(sent)

    def finish_kv(p):
        cols = slice(p * wide, (p + 1) * wide)
        for a, out in ((0, dk_out), (1, dv_out)):
            fars[p][a].wait_recv()
            out[:, cols] = (kept[a, p] + far_in[a, p].astype(F32)).astype(BF16)

    mix(0)
    mix(1)
    cross(0)
    cross_kv(0)
    mix(2)
    cross(1)
    along(0)
    mix(3)
    cross(2)
    along(1)
    cross_kv(1)
    finish_kv(0)
    cross(3)
    along(2)
    finish_kv(1)
    along(3)
    for p in range(PARTS):
        total = x_keep[p, z]
        for n in range(3):
            z_flow[p][n].wait_recv()
            total += z_in[p, n].astype(F32)
        proj[p * PART_ROWS : (p + 1) * PART_ROWS, :] = total
    flows.finish()


def reduce(dk, dv, att, att_t, grad, grad_twin, resid, w_all):
    n_ctx = lax.axis_size("ctx")
    seq, kv_cols = dk.shape
    rows, feats = att.shape
    chunk = seq // n_ctx
    heads = att_t.shape[0]
    per = heads // n_ctx
    wide = kv_cols // PIECES
    hbm = pl.BlockSpec(memory_space=pltpu.HBM)
    vmem = pl.BlockSpec(memory_space=pltpu.VMEM)

    def quad(dtype, n=4, lanes=2 * HEAD_DIM):
        return pltpu.VMEM((PARTS, n, PART_ROWS, lanes), dtype)

    def kv_buf(height, dtype=BF16):
        return pltpu.VMEM((2, PIECES, height, wide), dtype)

    return pl.pallas_call(
        reduce_kernel,
        in_specs=[hbm, hbm, hbm, vmem, vmem, vmem, hbm, hbm],
        out_specs=[vmem] * 4,
        out_shape=[
            jax.ShapeDtypeStruct((rows, feats), BF16),
            jax.ShapeDtypeStruct((chunk, kv_cols), BF16),
            jax.ShapeDtypeStruct((chunk, kv_cols), BF16),
            jax.ShapeDtypeStruct((per * HEAD_DIM, HEAD_DIM), F32),
        ],
        scratch_shapes=[
            pltpu.VMEM(att_t.shape, BF16),
            pltpu.VMEM(w_all.shape, BF16),
            pltpu.VMEM(att.shape, BF16),
            pltpu.VMEM(resid.shape, BF16),
            pltpu.VMEM((2, 2 * chunk, kv_cols), BF16),
            pltpu.VMEM((2, 2 * chunk, kv_cols), BF16),
            kv_buf(2 * chunk),
            kv_buf(2 * chunk),
            kv_buf(2 * chunk),
            kv_buf(2 * chunk),
            kv_buf(chunk, F32),
            kv_buf(chunk),
            kv_buf(chunk),
            quad(BF16, 8),
            quad(F32, 8),
            quad(BF16),
            quad(BF16),
            quad(BF16),
            quad(BF16),
            quad(BF16),
            quad(BF16),
            quad(BF16),
            quad(BF16),
            quad(BF16),
            quad(BF16),
            pltpu.VMEM((PARTS, 3, 4, PART_ROWS, HEAD_DIM), BF16),
            pltpu.VMEM((PARTS, 3, 4, PART_ROWS, HEAD_DIM), BF16),
            quad(F32, 4, HEAD_DIM),
            quad(BF16, 3, HEAD_DIM),
            quad(BF16, 3, HEAD_DIM),
            pltpu.SemaphoreType.DMA((REDUCE_FLOWS,)),
            pltpu.SemaphoreType.DMA((REDUCE_FLOWS,)),
            pltpu.SemaphoreType.DMA((7,)),
        ],
        compiler_params=pltpu.CompilerParams(
            collective_id=1, has_side_effects=True, vmem_limit_bytes=50 << 20
        ),
        cost_estimate=pl.CostEstimate(
            flops=4 * rows * feats * feats, bytes_accessed=24 << 20, transcendentals=0
        ),
        name="reduce",
    )(dk, dv, att, att_t, grad, grad_twin, resid, w_all)


def local(queries, keys, values, resid, grad_out, w_out, block_list, block_count):
    grad = grad_out[0]
    kv, w_all, datt, grad_twin = gather(keys[0], values[0], grad, w_out)
    att, att_t, dq, dk, dv = attention(queries[0], datt, kv, block_list, block_count)
    mixed, dk, dv, proj = reduce(dk, dv, att, att_t, grad, grad_twin, resid[0], w_all)
    return mixed[None], dq[None], dk[None], dv[None], proj


def solution(mesh):
    rows = P("fsdp", "ctx", None)
    in_specs = (rows, rows, rows, rows, rows, P(None, "fsdp"), P("ctx", None), P("ctx"))
    out_specs = (rows, rows, rows, rows, P("ctx", "fsdp"))
    return jax.shard_map(local, mesh=mesh, in_specs=in_specs, out_specs=out_specs, check_vma=False)
```

```python
import functools
import itertools
import math

import jax
import jax.numpy as jnp
from jax import lax
from jax.experimental import pallas as pl
from jax.experimental.pallas import tpu as pltpu
from jax.sharding import PartitionSpec as P

QUERY_HEADS = 16
KV_HEADS = 4
GROUP = QUERY_HEADS // KV_HEADS
HEAD_DIM = 128
BLOCK = 128
SLOTS = 8
STEP = 4
SCALE = 1.0 / math.sqrt(HEAD_DIM)
BF16 = jnp.bfloat16
F32 = jnp.float32
LOG2E = math.log2(math.e)
MESH = pl.DeviceIdType.MESH


def dot(a, b, ca, cb):
    return lax.dot_general(a, b, (((ca,), (cb,)), ((), ())), preferred_element_type=F32)


def stack_heads(ref, i):
    rows = slice(i * BLOCK, (i + 1) * BLOCK)
    return jnp.concatenate(
        [ref[rows, h * HEAD_DIM : (h + 1) * HEAD_DIM] for h in range(GROUP)], axis=0
    )


def attention_kernel(
    list_ref, count_ref, q_ref, do_ref, k_ref, v_ref,
    att_ref, att_t_ref, dq_ref, dk_ref, dv_ref, dk_acc, dv_acc,
):
    cols = GROUP * BLOCK
    count = q_ref.shape[0] // BLOCK
    dk_acc[...] = jnp.zeros_like(dk_acc)
    dv_acc[...] = jnp.zeros_like(dv_acc)

    def slots(ns):
        key_pos = lax.broadcasted_iota(jnp.int32, (BLOCK, cols), 0)
        query_pos = lax.broadcasted_iota(jnp.int32, (BLOCK, cols), 1) % BLOCK
        rows, k_sel, v_sel, qs, dos = [], [], [], [], []
        for i, n in enumerate(ns):
            rows.append(
                [pl.ds(pl.multiple_of(list_ref[i, j] * BLOCK, BLOCK), BLOCK) for j in range(n)]
            )
            k_sel.append(jnp.concatenate([k_ref[0, r, :] for r in rows[i]], axis=0))
            v_sel.append(jnp.concatenate([v_ref[0, r, :] for r in rows[i]], axis=0))
            qs.append(stack_heads(q_ref, i))
            dos.append(stack_heads(do_ref, i))
        scores = [dot(k, q, 1, 1) for k, q in zip(k_sel, qs)]
        prob_grads = [dot(v, do, 1, 1) for v, do in zip(v_sel, dos)]
        probs, rounded = [], []
        for i, (s, n) in enumerate(zip(scores, ns)):
            parts = [jnp.where(key_pos <= query_pos, s[:BLOCK], -1e30)]
            if n > STEP:
                parts.append(s[BLOCK : (n - STEP + 1) * BLOCK])
            for j in range(n - STEP + 1, n):
                dead = jnp.where(j < count_ref[i], 0.0, -1e30).astype(F32)
                parts.append(s[j * BLOCK : (j + 1) * BLOCK] + dead)
            s = jnp.concatenate(parts, axis=0)
            top = jnp.max(s, axis=0, keepdims=True)
            e = jnp.exp2((s - top) * (SCALE * LOG2E))
            p = e * (1.0 / jnp.sum(e, axis=0, keepdims=True))
            probs.append(p)
            rounded.append(p.astype(BF16))
        outs = [dot(v, pb, 0, 0).astype(BF16) for v, pb in zip(v_sel, rounded)]
        row_dots = [
            jnp.sum(o.astype(F32) * do.T.astype(F32), axis=0, keepdims=True)
            for o, do in zip(outs, dos)
        ]
        grads = [
            (p * (dp - r)).astype(BF16) for p, dp, r in zip(probs, prob_grads, row_dots)
        ]
        dqs = [(dot(k, ds, 0, 0) * SCALE).astype(BF16).T for k, ds in zip(k_sel, grads)]
        dks = [dot(ds, q, 1, 0) for ds, q in zip(grads, qs)]
        dvs = [dot(pb, do, 1, 0) for pb, do in zip(rounded, dos)]
        for i, (o_t, dq) in enumerate(zip(outs, dqs)):
            o = o_t.T
            mine = slice(i * BLOCK, (i + 1) * BLOCK)
            for h in range(GROUP):
                lanes = slice(h * HEAD_DIM, (h + 1) * HEAD_DIM)
                here = slice(h * BLOCK, (h + 1) * BLOCK)
                att_ref[mine, lanes] = o[here]
                dq_ref[mine, lanes] = dq[here]
                att_t_ref[h, :, mine] = o_t[:, here]
        for i, n in enumerate(ns):
            for j in range(n):
                here = slice(j * BLOCK, (j + 1) * BLOCK)
                dk_acc[rows[i][j], :] += dks[i][here]
                dv_acc[rows[i][j], :] += dvs[i][here]

    need = [(count_ref[i] + STEP - 1) // STEP for i in range(count)]
    for ns in itertools.product(range(STEP, SLOTS + 1, STEP), repeat=count):
        hit = functools.reduce(
            jnp.logical_and, [have == n // STEP for have, n in zip(need, ns)]
        )
        pl.when(hit)(functools.partial(slots, ns))

    dk_ref[...] = (dk_acc[...] * SCALE).astype(BF16)
    dv_ref[...] = dv_acc[...].astype(BF16)


def attention(queries, datt, kv, block_list, block_count):
    rows, width = queries.shape
    seq = kv.shape[1]
    group_cols = GROUP * HEAD_DIM
    kv_cols = KV_HEADS * HEAD_DIM
    q_spec = pl.BlockSpec((rows, group_cols), lambda g, *_: (0, g))

    def kv_spec(which):
        return pl.BlockSpec((1, seq, HEAD_DIM), lambda g, *_: (which, 0, g))

    out_spec = pl.BlockSpec((seq, HEAD_DIM), lambda g, *_: (0, g))
    t_spec = pl.BlockSpec((GROUP, HEAD_DIM, rows), lambda g, *_: (g, 0, 0))
    flops = 12 * rows * QUERY_HEADS * SLOTS * BLOCK * HEAD_DIM
    return pl.pallas_call(
        attention_kernel,
        grid_spec=pltpu.PrefetchScalarGridSpec(
            num_scalar_prefetch=2,
            grid=(KV_HEADS,),
            in_specs=[q_spec, q_spec, kv_spec(0), kv_spec(1)],
            out_specs=[q_spec, t_spec, q_spec, out_spec, out_spec],
            scratch_shapes=[pltpu.VMEM((seq, HEAD_DIM), F32)] * 2,
        ),
        out_shape=[
            jax.ShapeDtypeStruct((rows, width), BF16),
            jax.ShapeDtypeStruct((QUERY_HEADS, HEAD_DIM, rows), BF16),
            jax.ShapeDtypeStruct((rows, width), BF16),
            jax.ShapeDtypeStruct((seq, kv_cols), BF16),
            jax.ShapeDtypeStruct((seq, kv_cols), BF16),
        ],
        compiler_params=pltpu.CompilerParams(
            dimension_semantics=("arbitrary",), vmem_limit_bytes=44 << 20
        ),
        cost_estimate=pl.CostEstimate(
            flops=flops, bytes_accessed=12 << 20, transcendentals=rows * QUERY_HEADS * SLOTS * BLOCK
        ),
        name="attention",
    )(block_list, block_count, queries, datt, kv, kv)


def mesh_spot():
    c, f = lax.axis_index("ctx"), lax.axis_index("fsdp")
    return c, f, c // 2, lax.rem(c, 2), f // 4, lax.rem(f // 2, 2), lax.rem(f, 2)


def neighbours():
    c, f, z, xh, y, xl, k = mesh_spot()
    z_up, z_down = lax.rem(z + 1, 4), lax.rem(z + 3, 4)
    y_up, y_down = lax.rem(y + 1, 4), lax.rem(y + 3, 4)
    side, far, twin = 4 * y + 2 * (1 - xl) + k, 2 * z + 1 - xh, 4 * y + 2 * xl + 1 - k
    return dict(
        far=(far, f),
        near=(c, side),
        back=(far, side),
        twin=(c, twin),
        z_up=(2 * z_up + xh, f),
        z_down=(2 * z_down + xh, f),
        y_up=(c, 4 * y_up + 2 * xl + k),
        y_down=(c, 4 * y_down + 2 * xl + k),
    )


def meet(peers):
    barrier = pltpu.get_barrier_semaphore()
    for peer in peers:
        pl.semaphore_signal(barrier, inc=1, device_id=peer, device_id_type=MESH)
    pl.semaphore_wait(barrier, len(peers))


def act_if(condition, act):
    def run():
        act()

    if condition is None:
        run()
    else:
        pl.when(condition)(run)


class Sent:
    def __init__(self, copy, gives, takes):
        self.copy, self.gives, self.takes = copy, gives, takes

    def wait_recv(self):
        act_if(self.takes, self.copy.wait_recv)

    def wait_send(self):
        act_if(self.gives, self.copy.wait_send)


class Flows:
    def __init__(self, send_sem, recv_sem):
        self.send_sem, self.recv_sem, self.made = send_sem, recv_sem, []

    def send(self, src, dst, peer, gives=None, takes=None):
        n = len(self.made)
        copy = pltpu.make_async_remote_copy(
            src_ref=src,
            dst_ref=dst,
            send_sem=self.send_sem.at[n],
            recv_sem=self.recv_sem.at[n],
            device_id=peer,
            device_id_type=MESH,
        )
        act_if(gives, copy.start)
        self.made.append(Sent(copy, gives, takes))
        return self.made[-1]

    def finish(self):
        for copy in self.made:
            copy.wait_send()


GATHER_FLOWS = 40


def gather_kernel(
    keys, values, grad, w, kv, w_all, datt, grad_twin, w_buf, total, send_sem, recv_sem, here_sem
):
    c, f, z, xh, y, xl, k = mesh_spot()
    at = neighbours()
    z_up, z_down, z_far = lax.rem(z + 1, 4), lax.rem(z + 3, 4), lax.rem(z + 2, 4)
    y_up, y_down, y_far = lax.rem(y + 1, 4), lax.rem(y + 3, 4), lax.rem(y + 2, 4)
    rows = keys.shape[0]
    half = w.shape[0] // 2
    meet(list(at.values()))
    flows = Flows(send_sem, recv_sem)

    def chunk(a, who):
        return kv.at[a, pl.ds(pl.multiple_of(who * rows, rows), rows), :]

    def shard(yy, xx, kk):
        return 4 * yy + 2 * xx + kk

    def whole(who):
        return w_buf.at[who]

    def part(who, p):
        return w_buf.at[who, pl.ds(p * half, half), :]

    own = (keys, values)
    up = dict(gives=z < 3, takes=z_down < 3)
    down = (dict(gives=z < 1, takes=z_up < 1), dict(gives=z < 2, takes=z_up < 2))
    on_up = dict(gives=(z == 1) | (z == 2), takes=z >= 2)
    on_down = dict(gives=(z == 0) | (z == 3), takes=z >= 2)
    later = dict(gives=z >= 2, takes=z >= 2)
    w_side = [
        flows.send(w.at[pl.ds(p * half, half), :], part(f, p), at[("near", "back")[p]])
        for p in (0, 1)
    ]
    w_up = flows.send(w, whole(f), at["y_up"])
    w_down = flows.send(w, whole(f), at["y_down"])
    kv_up = [flows.send(own[a], chunk(a, c), at["z_up"], **up) for a in (0, 1)]
    kv_down = [flows.send(own[a], chunk(a, c), at["z_down"], **down[a]) for a in (1, 0)][::-1]
    kv_far = [flows.send(own[a], chunk(a, c), at["far"]) for a in (0, 1)]
    to_twin = [flows.send(w, whole(f), at["twin"])]
    swap = flows.send(grad, grad_twin, at["twin"])
    here = [
        pltpu.make_async_copy(keys, chunk(0, c), here_sem.at[0]),
        pltpu.make_async_copy(values, chunk(1, c), here_sem.at[1]),
        pltpu.make_async_copy(w, whole(f), here_sem.at[2]),
    ]
    for copy in here:
        copy.start()

    side = shard(y, 1 - xl, k)
    side_up, side_down = [], []

    def pass_side(p):
        w_side[p].wait_recv()
        side_up.append(flows.send(part(side, p), part(side, p), at["y_up"]))
        side_down.append(flows.send(part(side, p), part(side, p), at["y_down"]))

    pass_side(0)
    kv_up[0].wait_recv()
    got_k = 2 * z_down + xh
    on_k = flows.send(chunk(0, got_k), chunk(0, got_k), at["z_up"], **on_up)
    kv_down[1].wait_recv()
    got_v = 2 * z_up + xh
    on_v = flows.send(chunk(1, got_v), chunk(1, got_v), at["z_down"], **on_down)
    w_up.wait_recv()
    got = shard(y_down, xl, k)
    on_w0 = flows.send(part(got, 0), part(got, 0), at["y_up"])
    to_twin.append(flows.send(whole(got), whole(got), at["twin"]))
    w_down.wait_recv()
    got = shard(y_up, xl, k)
    on_w1 = flows.send(part(got, 1), part(got, 1), at["y_down"])
    to_twin.append(flows.send(whole(got), whole(got), at["twin"]))
    pass_side(1)
    to_twin.append(flows.send(whole(side), whole(side), at["twin"]))

    other = 2 * z + 1 - xh
    pair_up, pair_down = [None, None], [None, None]
    for a in (0, 1):
        kv_far[a].wait_recv()
        pair_up[a] = flows.send(chunk(a, other), chunk(a, other), at["z_up"], **up)
        pair_down[a] = flows.send(chunk(a, other), chunk(a, other), at["z_down"], **down[a])

    def multiply(yy, n):
        slab = pl.ds(pl.multiple_of(4 * yy, 4), 4)
        out = pltpu.make_async_copy(w_buf.at[slab], w_all.at[slab], here_sem.at[3 + n])
        out.start()
        here.append(out)

        def columns(b, carry):
            lanes = pl.ds(pl.multiple_of(b * 512, 512), 512)
            out = None
            for s in (0, 2):
                who = 4 * yy + s
                g = grad[:, pl.ds(pl.multiple_of(who * HEAD_DIM, 2 * HEAD_DIM), 2 * HEAD_DIM)]
                both = jnp.concatenate([w_buf[who, lanes, :], w_buf[who + 1, lanes, :]], axis=1)
                term = dot(g, both, 1, 1)
                out = term if out is None else out + term
            total[:, lanes] = out if n == 0 else total[:, lanes] + out
            return carry

        lax.fori_loop(0, total.shape[1] // 512, columns, 0)

    here.pop().wait()
    for n in (0, 3):
        to_twin[n].wait_recv()
    multiply(y, 0)

    def piece(a, who, p):
        start = pl.multiple_of(who * rows, rows) + p * (rows // 2)
        return kv.at[a, pl.ds(start, rows // 2), :]

    on_k.wait_recv()
    got = 2 * z_far + xh
    cross_k = flows.send(piece(0, got, 1), piece(0, got, 1), at["far"], **later)
    on_v.wait_recv()
    cross_v = flows.send(piece(1, got, 1), piece(1, got, 1), at["far"], **later)
    got = shard(y_far, xl, k)
    on_w0.wait_recv()
    on_s0 = flows.send(part(got, 0), part(got, 0), at["near"])
    to_twin.append(flows.send(part(got, 0), part(got, 0), at["twin"]))
    on_w1.wait_recv()
    on_s1 = flows.send(part(got, 1), part(got, 1), at["back"])
    to_twin.append(flows.send(part(got, 1), part(got, 1), at["twin"]))

    pair_up[0].wait_recv()
    got = 2 * z_down + 1 - xh
    pair_on_k = flows.send(piece(0, got, 0), piece(0, got, 0), at["z_up"], **on_up)
    pair_down[1].wait_recv()
    got = 2 * z_up + 1 - xh
    pair_on_v = flows.send(piece(1, got, 0), piece(1, got, 0), at["z_down"], **on_down)

    for yy, arrived in ((y_down, side_up), (y_up, side_down)):
        got = shard(yy, 1 - xl, k)
        for copy in arrived:
            copy.wait_recv()
        to_twin.append(flows.send(whole(got), whole(got), at["twin"]))
    got = shard(y_far, 1 - xl, k)
    on_s0.wait_recv()
    to_twin.append(flows.send(part(got, 0), part(got, 0), at["twin"]))
    on_s1.wait_recv()
    to_twin.append(flows.send(part(got, 1), part(got, 1), at["twin"]))
    for n in (1, 6):
        to_twin[n].wait_recv()
    multiply(y_down, 1)
    for n in (2, 7):
        to_twin[n].wait_recv()
    multiply(y_up, 2)
    for n in (4, 5, 8, 9):
        to_twin[n].wait_recv()
    multiply(y_far, 3)
    datt[...] = total[...].astype(BF16)
    for copy in (swap, kv_up[1], kv_down[0], pair_up[1], pair_down[0]):
        copy.wait_recv()
    for copy in (cross_k, cross_v, pair_on_k, pair_on_v):
        copy.wait_recv()
    flows.finish()
    for copy in here:
        copy.wait()


def gather(keys, values, grad, w):
    rows, kv_cols = keys.shape
    feats, cols = w.shape
    n_ctx, n_fsdp = lax.axis_size("ctx"), lax.axis_size("fsdp")
    hbm = pl.BlockSpec(memory_space=pltpu.HBM)
    vmem = pl.BlockSpec(memory_space=pltpu.VMEM)
    return pl.pallas_call(
        gather_kernel,
        in_specs=[hbm, hbm, vmem, hbm],
        out_specs=[hbm, hbm, vmem, hbm],
        out_shape=[
            jax.ShapeDtypeStruct((2, n_ctx * rows, kv_cols), BF16),
            jax.ShapeDtypeStruct((n_fsdp, feats, cols), BF16),
            jax.ShapeDtypeStruct((rows, feats), BF16),
            jax.ShapeDtypeStruct(grad.shape, BF16),
        ],
        scratch_shapes=[
            pltpu.VMEM((n_fsdp, feats, cols), BF16),
            pltpu.VMEM((rows, feats), F32),
            pltpu.SemaphoreType.DMA((GATHER_FLOWS,)),
            pltpu.SemaphoreType.DMA((GATHER_FLOWS,)),
            pltpu.SemaphoreType.DMA((7,)),
        ],
        compiler_params=pltpu.CompilerParams(
            collective_id=0, has_side_effects=True, vmem_limit_bytes=60 << 20
        ),
        cost_estimate=pl.CostEstimate(
            flops=2 * rows * feats * feats, bytes_accessed=24 << 20, transcendentals=0
        ),
        name="gather",
    )(keys, values, grad, w)


REDUCE_FLOWS = 66
PIECES = 2
PARTS = 4
PART_ROWS = 2 * HEAD_DIM // PARTS


def reduce_kernel(
    dk, dv, att, att_t, grad, grad_twin, resid, w_all,
    mixed, dk_out, dv_out, proj,
    att_twin, w_buf, res_buf, ahead, mine, hop_in, raw_in, sum_in, sum_out, kept, far_out, far_in,
    far_p, own_keep, up_raw, down_raw, top_in, low_in, top_out, low_out,
    top_raw, low_raw, top_sum, low_sum, x_out, x_in, x_keep, z_out, z_in,
    send_sem, recv_sem, here_sem,
):
    c, f, z, xh, y, xl, k = mesh_spot()
    at = neighbours()
    z_up, z_down, z_far = lax.rem(z + 1, 4), lax.rem(z + 3, 4), lax.rem(z + 2, 4)
    y_up, y_down, y_far = lax.rem(y + 1, 4), lax.rem(y + 3, 4), lax.rem(y + 2, 4)
    at["z_far"] = (2 * z_far + xh, f)
    rows, kv_cols = dk_out.shape
    pair = 2 * rows
    wide = kv_cols // PIECES
    meet(list(at.values()))
    flows = Flows(send_sem, recv_sem)
    parts = (dk, dv)

    def block(a, zz, p):
        return parts[a].at[
            pl.ds(pl.multiple_of(zz * pair, pair), pair), pl.ds(p * wide, wide)
        ]

    swap = flows.send(att_t, att_twin, at["twin"])
    hop_in_k, hop_in_v = z_down >= 2, z_up >= 2
    raw_in_k, raw_in_v = z_up >= 1, z_down == 3
    sum_in_k, sum_in_v = (z_down == 3) | (z_down == 0), z_up >= 1
    for buffer, a, comes in (
        (hop_in, 0, hop_in_k),
        (hop_in, 1, hop_in_v),
        (raw_in, 0, raw_in_k),
        (raw_in, 1, raw_in_v),
        (sum_in, 0, sum_in_k),
        (sum_in, 1, sum_in_v),
    ):

        def clear(buffer=buffer, a=a):
            buffer[a] = jnp.zeros_like(buffer[a])

        pl.when(jnp.logical_not(comes))(clear)
    hops = [
        [
            flows.send(block(0, z_far, p), hop_in.at[0, p], at["z_up"], z >= 2, hop_in_k),
            flows.send(block(1, z_far, p), hop_in.at[1, p], at["z_down"], z >= 2, hop_in_v),
        ]
        for p in range(PIECES)
    ]
    here = []
    for n, (src, dst) in enumerate(
        [
            (dk.at[pl.ds(pl.multiple_of(z_up * pair, pair), pair), :], ahead.at[0]),
            (dv.at[pl.ds(pl.multiple_of(z_down * pair, pair), pair), :], ahead.at[1]),
            (dk.at[pl.ds(pl.multiple_of(z * pair, pair), pair), :], mine.at[0]),
            (dv.at[pl.ds(pl.multiple_of(z * pair, pair), pair), :], mine.at[1]),
            (w_all, w_buf),
            (resid, res_buf),
        ]
    ):
        copy = pltpu.make_async_copy(src, dst, here_sem.at[n])
        copy.start()
        here.append(copy)

    def product(yy, p, low):
        lanes = [
            pl.ds(pl.multiple_of((4 * yy + 2 * s + k) * HEAD_DIM, HEAD_DIM), HEAD_DIM)
            for s in (0, 1)
        ]
        first, of = p % (PARTS // 2) * PART_ROWS, p // (PARTS // 2)

        def term(left, right):
            heads = [left[2 * (m + low) + of, first : first + PART_ROWS] for m in range(4)]
            wide = jnp.concatenate([right[:, s] for s in lanes], axis=1)
            return dot(jnp.concatenate(heads, axis=0), wide, 1, 0)

        out = term(att_t, grad) + term(att_twin, grad_twin)
        return out.reshape(4, PART_ROWS, 2 * HEAD_DIM)

    swap.wait_recv()
    top_hop, low_hop = [], []
    for p in range(PARTS):
        far_p[p, 0:4] = product(y_far, p, 0).astype(BF16)
        top_hop.append(flows.send(far_p.at[p, pl.ds(0, 4)], top_in.at[p], at["y_up"]))
        far_p[p, 4:8] = product(y_far, p, 4).astype(BF16)
        low_hop.append(flows.send(far_p.at[p, pl.ds(4, 4)], low_in.at[p], at["y_down"]))
    for copy in here[:4]:
        copy.wait()
    raws, sums = [], []
    raw_top, raw_low, top_on, low_on = [], [], [], []

    def relay_kv(p):
        cols = slice(p * wide, (p + 1) * wide)
        raws.append(
            [
                flows.send(block(0, z_down, p), raw_in.at[0, p], at["z_down"], z >= 1, raw_in_k),
                flows.send(block(1, z_up, p), raw_in.at[1, p], at["z_up"], z == 3, raw_in_v),
            ]
        )
        sums.append([])
        for a, towards, gives, takes in (
            (0, "z_up", (z == 3) | (z == 0), sum_in_k),
            (1, "z_down", z >= 1, sum_in_v),
        ):
            hops[p][a].wait_recv()
            sum_out[a, p] = (ahead[a, :, cols].astype(F32) + hop_in[a, p].astype(F32)).astype(BF16)
            sums[p].append(
                flows.send(sum_out.at[a, p], sum_in.at[a, p], at[towards], gives, takes)
            )

    for p in range(PARTS):
        up_raw[p] = product(y_up, p, 4).astype(BF16)
        raw_low.append(flows.send(up_raw.at[p], low_raw.at[p], at["y_up"]))
        down_raw[p] = product(y_down, p, 0).astype(BF16)
        raw_top.append(flows.send(down_raw.at[p], top_raw.at[p], at["y_down"]))
        keep = product(y_up, p, 0)
        top_hop[p].wait_recv()
        top_out[p] = (keep + top_in[p].astype(F32)).astype(BF16)
        top_on.append(flows.send(top_out.at[p], top_sum.at[p], at["y_up"]))
        keep = product(y_down, p, 4)
        low_hop[p].wait_recv()
        low_out[p] = (keep + low_in[p].astype(F32)).astype(BF16)
        low_on.append(flows.send(low_out.at[p], low_sum.at[p], at["y_down"]))
        if p % 2:
            relay_kv(p // 2)
    for p in range(PARTS):
        own_keep[p, 0:4] = product(y, p, 0)
        own_keep[p, 4:8] = product(y, p, 4)

    for copy in here[4:]:
        copy.wait()

    def project(n, carry):
        lanes = pl.ds(pl.multiple_of(n * 2 * HEAD_DIM, 2 * HEAD_DIM), 2 * HEAD_DIM)
        both = jnp.concatenate([w_buf[2 * n], w_buf[2 * n + 1]], axis=1)
        out = dot(att[...], both, 1, 0)
        mixed[:, lanes] = (res_buf[:, lanes].astype(F32) + out).astype(BF16)
        return carry

    def mix(quarter):
        many = w_buf.shape[0] // 8
        lax.fori_loop(quarter * many, (quarter + 1) * many, project, 0)

    keep_rows = pl.ds(pl.multiple_of(xh * rows, rows), rows)
    give_rows = pl.ds(pl.multiple_of((1 - xh) * rows, rows), rows)
    fars, x_flow, z_flow = [], [], []
    x_to = ("near", "far", "back")
    z_to = (("z_up", z_up), ("z_down", z_down), ("z_far", z_far))
    near_lanes = pl.ds(pl.multiple_of((1 - xl) * HEAD_DIM, HEAD_DIM), HEAD_DIM)
    own_lanes = pl.ds(pl.multiple_of(xl * HEAD_DIM, HEAD_DIM), HEAD_DIM)

    def cross_kv(p):
        cols = pl.ds(p * wide, wide)
        fars.append([])
        for a in (0, 1):
            raws[p][a].wait_recv()
            sums[p][a].wait_recv()

            def gathered(which):
                return (
                    mine[a, which, cols].astype(F32)
                    + raw_in[a, p, which, :].astype(F32)
                    + sum_in[a, p, which, :].astype(F32)
                )

            far_out[a, p] = gathered(give_rows).astype(BF16)
            fars[p].append(flows.send(far_out.at[a, p], far_in.at[a, p], at["far"]))
            kept[a, p] = gathered(keep_rows)

    def cross(p):
        raw_top[p].wait_recv()
        top_on[p].wait_recv()
        raw_low[p].wait_recv()
        low_on[p].wait_recv()
        for m in range(4):
            own_keep[p, m] += top_raw[p, m].astype(F32) + top_sum[p, m].astype(F32)
            own_keep[p, m + 4] += low_raw[p, m].astype(F32) + low_sum[p, m].astype(F32)
        sent = []
        for n, (hi, lanes) in enumerate(
            ((xh, near_lanes), (1 - xh, own_lanes), (1 - xh, near_lanes))
        ):
            for zz in range(4):
                x_out[p, n, zz] = own_keep[p, 2 * zz + hi, :, lanes].astype(BF16)
            sent.append(flows.send(x_out.at[p, n], x_in.at[p, n], at[x_to[n]]))
        x_flow.append(sent)

    def along(p):
        for n in range(3):
            x_flow[p][n].wait_recv()
        for zz in range(4):
            total = own_keep[p, 2 * zz + xh, :, own_lanes]
            for n in range(3):
                total += x_in[p, n, zz].astype(F32)
            x_keep[p, zz] = total
        sent = []
        for n, (name, zz) in enumerate(z_to):
            z_out[p, n] = x_keep[p, zz].astype(BF16)
            sent.append(flows.send(z_out.at[p, n], z_in.at[p, n], at[name]))
        z_flow.append(sent)

    def finish_kv(p):
        cols = slice(p * wide, (p + 1) * wide)
        for a, out in ((0, dk_out), (1, dv_out)):
            fars[p][a].wait_recv()
            out[:, cols] = (kept[a, p] + far_in[a, p].astype(F32)).astype(BF16)

    mix(0)
    mix(1)
    cross(0)
    cross_kv(0)
    mix(2)
    cross(1)
    along(0)
    mix(3)
    cross(2)
    along(1)
    cross_kv(1)
    finish_kv(0)
    cross(3)
    along(2)
    finish_kv(1)
    along(3)
    for p in range(PARTS):
        total = x_keep[p, z]
        for n in range(3):
            z_flow[p][n].wait_recv()
            total += z_in[p, n].astype(F32)
        proj[p * PART_ROWS : (p + 1) * PART_ROWS, :] = total
    flows.finish()


def reduce(dk, dv, att, att_t, grad, grad_twin, resid, w_all):
    n_ctx = lax.axis_size("ctx")
    seq, kv_cols = dk.shape
    rows, feats = att.shape
    chunk = seq // n_ctx
    heads = att_t.shape[0]
    per = heads // n_ctx
    wide = kv_cols // PIECES
    hbm = pl.BlockSpec(memory_space=pltpu.HBM)
    vmem = pl.BlockSpec(memory_space=pltpu.VMEM)

    def quad(dtype, n=4, lanes=2 * HEAD_DIM):
        return pltpu.VMEM((PARTS, n, PART_ROWS, lanes), dtype)

    def kv_buf(height, dtype=BF16):
        return pltpu.VMEM((2, PIECES, height, wide), dtype)

    return pl.pallas_call(
        reduce_kernel,
        in_specs=[hbm, hbm, vmem, vmem, vmem, vmem, hbm, hbm],
        out_specs=[vmem] * 4,
        out_shape=[
            jax.ShapeDtypeStruct((rows, feats), BF16),
            jax.ShapeDtypeStruct((chunk, kv_cols), BF16),
            jax.ShapeDtypeStruct((chunk, kv_cols), BF16),
            jax.ShapeDtypeStruct((per * HEAD_DIM, HEAD_DIM), F32),
        ],
        scratch_shapes=[
            pltpu.VMEM(att_t.shape, BF16),
            pltpu.VMEM(w_all.shape, BF16),
            pltpu.VMEM(resid.shape, BF16),
            pltpu.VMEM((2, 2 * chunk, kv_cols), BF16),
            pltpu.VMEM((2, 2 * chunk, kv_cols), BF16),
            kv_buf(2 * chunk),
            kv_buf(2 * chunk),
            kv_buf(2 * chunk),
            kv_buf(2 * chunk),
            kv_buf(chunk, F32),
            kv_buf(chunk),
            kv_buf(chunk),
            quad(BF16, 8),
            quad(F32, 8),
            quad(BF16),
            quad(BF16),
            quad(BF16),
            quad(BF16),
            quad(BF16),
            quad(BF16),
            quad(BF16),
            quad(BF16),
            quad(BF16),
            quad(BF16),
            pltpu.VMEM((PARTS, 3, 4, PART_ROWS, HEAD_DIM), BF16),
            pltpu.VMEM((PARTS, 3, 4, PART_ROWS, HEAD_DIM), BF16),
            quad(F32, 4, HEAD_DIM),
            quad(BF16, 3, HEAD_DIM),
            quad(BF16, 3, HEAD_DIM),
            pltpu.SemaphoreType.DMA((REDUCE_FLOWS,)),
            pltpu.SemaphoreType.DMA((REDUCE_FLOWS,)),
            pltpu.SemaphoreType.DMA((6,)),
        ],
        compiler_params=pltpu.CompilerParams(
            collective_id=1, has_side_effects=True, vmem_limit_bytes=40 << 20
        ),
        cost_estimate=pl.CostEstimate(
            flops=4 * rows * feats * feats, bytes_accessed=24 << 20, transcendentals=0
        ),
        name="reduce",
    )(dk, dv, att, att_t, grad, grad_twin, resid, w_all)


def local(queries, keys, values, resid, grad_out, w_out, block_list, block_count):
    grad = grad_out[0]
    kv, w_all, datt, grad_twin = gather(keys[0], values[0], grad, w_out)
    att, att_t, dq, dk, dv = attention(queries[0], datt, kv, block_list, block_count)
    mixed, dk, dv, proj = reduce(dk, dv, att, att_t, grad, grad_twin, resid[0], w_all)
    return mixed[None], dq[None], dk[None], dv[None], proj


def solution(mesh):
    rows = P("fsdp", "ctx", None)
    in_specs = (rows, rows, rows, rows, rows, P(None, "fsdp"), P("ctx", None), P("ctx"))
    out_specs = (rows, rows, rows, rows, P("ctx", "fsdp"))
    return jax.shard_map(local, mesh=mesh, in_specs=in_specs, out_specs=out_specs, check_vma=False)
```

```python
import functools
import itertools
import math

import jax
import jax.numpy as jnp
from jax import lax
from jax.experimental import pallas as pl
from jax.experimental.pallas import tpu as pltpu
from jax.sharding import PartitionSpec as P

QUERY_HEADS = 16
KV_HEADS = 4
GROUP = QUERY_HEADS // KV_HEADS
HEAD_DIM = 128
BLOCK = 128
SLOTS = 8
STEP = 4
SCALE = 1.0 / math.sqrt(HEAD_DIM)
BF16 = jnp.bfloat16
F32 = jnp.float32
LOG2E = math.log2(math.e)
MESH = pl.DeviceIdType.MESH


def dot(a, b, ca, cb):
    return lax.dot_general(a, b, (((ca,), (cb,)), ((), ())), preferred_element_type=F32)


def stack_heads(ref, i):
    rows = slice(i * BLOCK, (i + 1) * BLOCK)
    return jnp.concatenate(
        [ref[rows, h * HEAD_DIM : (h + 1) * HEAD_DIM] for h in range(GROUP)], axis=0
    )


def attention_kernel(
    list_ref, count_ref, q_ref, do_ref, k_ref, v_ref,
    att_ref, att_t_ref, dq_ref, dk_ref, dv_ref, dk_acc, dv_acc,
):
    cols = GROUP * BLOCK
    count = q_ref.shape[0] // BLOCK
    dk_acc[...] = jnp.zeros_like(dk_acc)
    dv_acc[...] = jnp.zeros_like(dv_acc)

    def slots(ns):
        key_pos = lax.broadcasted_iota(jnp.int32, (BLOCK, cols), 0)
        query_pos = lax.broadcasted_iota(jnp.int32, (BLOCK, cols), 1) % BLOCK
        rows, k_sel, v_sel, qs, dos = [], [], [], [], []
        for i, n in enumerate(ns):
            rows.append(
                [pl.ds(pl.multiple_of(list_ref[i, j] * BLOCK, BLOCK), BLOCK) for j in range(n)]
            )
            k_sel.append(jnp.concatenate([k_ref[0, r, :] for r in rows[i]], axis=0))
            v_sel.append(jnp.concatenate([v_ref[0, r, :] for r in rows[i]], axis=0))
            qs.append(stack_heads(q_ref, i))
            dos.append(stack_heads(do_ref, i))
        scores = [dot(k, q, 1, 1) for k, q in zip(k_sel, qs)]
        prob_grads = [dot(v, do, 1, 1) for v, do in zip(v_sel, dos)]
        probs, rounded = [], []
        for i, (s, n) in enumerate(zip(scores, ns)):
            parts = [jnp.where(key_pos <= query_pos, s[:BLOCK], -1e30)]
            if n > STEP:
                parts.append(s[BLOCK : (n - STEP + 1) * BLOCK])
            for j in range(n - STEP + 1, n):
                dead = jnp.where(j < count_ref[i], 0.0, -1e30).astype(F32)
                parts.append(s[j * BLOCK : (j + 1) * BLOCK] + dead)
            s = jnp.concatenate(parts, axis=0)
            top = jnp.max(s, axis=0, keepdims=True)
            e = jnp.exp2((s - top) * (SCALE * LOG2E))
            p = e * (1.0 / jnp.sum(e, axis=0, keepdims=True))
            probs.append(p)
            rounded.append(p.astype(BF16))
        outs = [dot(v, pb, 0, 0).astype(BF16) for v, pb in zip(v_sel, rounded)]
        row_dots = [
            jnp.sum(o.astype(F32) * do.T.astype(F32), axis=0, keepdims=True)
            for o, do in zip(outs, dos)
        ]
        grads = [
            (p * (dp - r)).astype(BF16) for p, dp, r in zip(probs, prob_grads, row_dots)
        ]
        dqs = [(dot(k, ds, 0, 0) * SCALE).astype(BF16).T for k, ds in zip(k_sel, grads)]
        dks = [dot(ds, q, 1, 0) for ds, q in zip(grads, qs)]
        dvs = [dot(pb, do, 1, 0) for pb, do in zip(rounded, dos)]
        for i, (o_t, dq) in enumerate(zip(outs, dqs)):
            o = o_t.T
            mine = slice(i * BLOCK, (i + 1) * BLOCK)
            for h in range(GROUP):
                lanes = slice(h * HEAD_DIM, (h + 1) * HEAD_DIM)
                here = slice(h * BLOCK, (h + 1) * BLOCK)
                att_ref[mine, lanes] = o[here]
                dq_ref[mine, lanes] = dq[here]
                att_t_ref[h, :, mine] = o_t[:, here]
        for i, n in enumerate(ns):
            for j in range(n):
                here = slice(j * BLOCK, (j + 1) * BLOCK)
                dk_acc[rows[i][j], :] += dks[i][here]
                dv_acc[rows[i][j], :] += dvs[i][here]

    need = [(count_ref[i] + STEP - 1) // STEP for i in range(count)]
    for ns in itertools.product(range(STEP, SLOTS + 1, STEP), repeat=count):
        hit = functools.reduce(
            jnp.logical_and, [have == n // STEP for have, n in zip(need, ns)]
        )
        pl.when(hit)(functools.partial(slots, ns))

    dk_ref[...] = (dk_acc[...] * SCALE).astype(BF16)
    dv_ref[...] = dv_acc[...].astype(BF16)


def attention(queries, datt, kv, block_list, block_count):
    rows, width = queries.shape
    seq = kv.shape[1]
    group_cols = GROUP * HEAD_DIM
    kv_cols = KV_HEADS * HEAD_DIM
    q_spec = pl.BlockSpec((rows, group_cols), lambda g, *_: (0, g))

    def kv_spec(which):
        return pl.BlockSpec((1, seq, HEAD_DIM), lambda g, *_: (which, 0, g))

    out_spec = pl.BlockSpec((seq, HEAD_DIM), lambda g, *_: (0, g))
    t_spec = pl.BlockSpec((GROUP, HEAD_DIM, rows), lambda g, *_: (g, 0, 0))
    flops = 12 * rows * QUERY_HEADS * SLOTS * BLOCK * HEAD_DIM
    return pl.pallas_call(
        attention_kernel,
        grid_spec=pltpu.PrefetchScalarGridSpec(
            num_scalar_prefetch=2,
            grid=(KV_HEADS,),
            in_specs=[q_spec, q_spec, kv_spec(0), kv_spec(1)],
            out_specs=[q_spec, t_spec, q_spec, out_spec, out_spec],
            scratch_shapes=[pltpu.VMEM((seq, HEAD_DIM), F32)] * 2,
        ),
        out_shape=[
            jax.ShapeDtypeStruct((rows, width), BF16),
            jax.ShapeDtypeStruct((QUERY_HEADS, HEAD_DIM, rows), BF16),
            jax.ShapeDtypeStruct((rows, width), BF16),
            jax.ShapeDtypeStruct((seq, kv_cols), BF16),
            jax.ShapeDtypeStruct((seq, kv_cols), BF16),
        ],
        compiler_params=pltpu.CompilerParams(
            dimension_semantics=("arbitrary",), vmem_limit_bytes=44 << 20
        ),
        cost_estimate=pl.CostEstimate(
            flops=flops, bytes_accessed=12 << 20, transcendentals=rows * QUERY_HEADS * SLOTS * BLOCK
        ),
        name="attention",
    )(block_list, block_count, queries, datt, kv, kv)


def mesh_spot():
    c, f = lax.axis_index("ctx"), lax.axis_index("fsdp")
    return c, f, c // 2, lax.rem(c, 2), f // 4, lax.rem(f // 2, 2), lax.rem(f, 2)


def neighbours():
    c, f, z, xh, y, xl, k = mesh_spot()
    z_up, z_down = lax.rem(z + 1, 4), lax.rem(z + 3, 4)
    y_up, y_down = lax.rem(y + 1, 4), lax.rem(y + 3, 4)
    side, far, twin = 4 * y + 2 * (1 - xl) + k, 2 * z + 1 - xh, 4 * y + 2 * xl + 1 - k
    return dict(
        far=(far, f),
        near=(c, side),
        back=(far, side),
        twin=(c, twin),
        z_up=(2 * z_up + xh, f),
        z_down=(2 * z_down + xh, f),
        y_up=(c, 4 * y_up + 2 * xl + k),
        y_down=(c, 4 * y_down + 2 * xl + k),
    )


def meet(peers):
    barrier = pltpu.get_barrier_semaphore()
    for peer in peers:
        pl.semaphore_signal(barrier, inc=1, device_id=peer, device_id_type=MESH)
    pl.semaphore_wait(barrier, len(peers))


def act_if(condition, act):
    def run():
        act()

    if condition is None:
        run()
    else:
        pl.when(condition)(run)


class Sent:
    def __init__(self, copy, gives, takes):
        self.copy, self.gives, self.takes = copy, gives, takes

    def wait_recv(self):
        act_if(self.takes, self.copy.wait_recv)

    def wait_send(self):
        act_if(self.gives, self.copy.wait_send)


class Flows:
    def __init__(self, send_sem, recv_sem):
        self.send_sem, self.recv_sem, self.made = send_sem, recv_sem, []

    def send(self, src, dst, peer, gives=None, takes=None):
        n = len(self.made)
        copy = pltpu.make_async_remote_copy(
            src_ref=src,
            dst_ref=dst,
            send_sem=self.send_sem.at[n],
            recv_sem=self.recv_sem.at[n],
            device_id=peer,
            device_id_type=MESH,
        )
        act_if(gives, copy.start)
        self.made.append(Sent(copy, gives, takes))
        return self.made[-1]

    def finish(self):
        for copy in self.made:
            copy.wait_send()


GATHER_FLOWS = 41


def gather_kernel(
    keys, values, grad, w, kv, w_all, datt, grad_twin, w_buf, total, send_sem, recv_sem, here_sem
):
    c, f, z, xh, y, xl, k = mesh_spot()
    at = neighbours()
    z_up, z_down, z_far = lax.rem(z + 1, 4), lax.rem(z + 3, 4), lax.rem(z + 2, 4)
    y_up, y_down, y_far = lax.rem(y + 1, 4), lax.rem(y + 3, 4), lax.rem(y + 2, 4)
    rows = keys.shape[0]
    half = w.shape[0] // 2
    meet(list(at.values()))
    flows = Flows(send_sem, recv_sem)

    def chunk(a, who):
        return kv.at[a, pl.ds(pl.multiple_of(who * rows, rows), rows), :]

    def shard(yy, xx, kk):
        return 4 * yy + 2 * xx + kk

    def whole(who):
        return w_buf.at[who]

    def part(who, p):
        return w_buf.at[who, pl.ds(p * half, half), :]

    own = (keys, values)
    up = dict(gives=z < 3, takes=z_down < 3)
    down = (dict(gives=z < 1, takes=z_up < 1), dict(gives=z < 2, takes=z_up < 2))
    on_up = dict(gives=(z == 1) | (z == 2), takes=z >= 2)
    on_down = dict(gives=(z == 0) | (z == 3), takes=z >= 2)
    later = dict(gives=z >= 2, takes=z >= 2)
    across = dict(gives=(z < 3) | (xh == 0), takes=(z < 3) | (xh == 1))
    w_side = [
        flows.send(w.at[pl.ds(p * half, half), :], part(f, p), at[("near", "back")[p]])
        for p in (0, 1)
    ]
    w_up = flows.send(w, whole(f), at["y_up"])
    w_down = flows.send(w, whole(f), at["y_down"])
    kv_up = [flows.send(own[a], chunk(a, c), at["z_up"], **up) for a in (0, 1)]
    kv_down = [flows.send(own[a], chunk(a, c), at["z_down"], **down[a]) for a in (1, 0)][::-1]
    kv_far = [flows.send(own[a], chunk(a, c), at["far"], **across) for a in (0, 1)]
    to_twin = [flows.send(w, whole(f), at["twin"])]
    swap = flows.send(grad, grad_twin, at["twin"])
    here = [
        pltpu.make_async_copy(keys, chunk(0, c), here_sem.at[0]),
        pltpu.make_async_copy(values, chunk(1, c), here_sem.at[1]),
        pltpu.make_async_copy(w, whole(f), here_sem.at[2]),
    ]
    for copy in here:
        copy.start()

    side = shard(y, 1 - xl, k)
    side_up, side_down = [], []

    def pass_side(p):
        w_side[p].wait_recv()
        side_up.append(flows.send(part(side, p), part(side, p), at["y_up"]))
        side_down.append(flows.send(part(side, p), part(side, p), at["y_down"]))

    pass_side(0)
    kv_up[0].wait_recv()
    got_k = 2 * z_down + xh
    on_k = flows.send(chunk(0, got_k), chunk(0, got_k), at["z_up"], **on_up)
    kv_down[1].wait_recv()
    got_v = 2 * z_up + xh
    on_v = flows.send(chunk(1, got_v), chunk(1, got_v), at["z_down"], **on_down)
    w_up.wait_recv()
    got = shard(y_down, xl, k)
    on_w0 = flows.send(part(got, 0), part(got, 0), at["y_up"])
    to_twin.append(flows.send(whole(got), whole(got), at["twin"]))
    w_down.wait_recv()
    got = shard(y_up, xl, k)
    on_w1 = flows.send(part(got, 1), part(got, 1), at["y_down"])
    to_twin.append(flows.send(whole(got), whole(got), at["twin"]))
    pass_side(1)
    to_twin.append(flows.send(whole(side), whole(side), at["twin"]))

    other = 2 * z + 1 - xh
    pair_up, pair_down = [None, None], [None, None]
    for a in (0, 1):
        kv_far[a].wait_recv()
        pair_up[a] = flows.send(chunk(a, other), chunk(a, other), at["z_up"], **up)
        pair_down[a] = flows.send(chunk(a, other), chunk(a, other), at["z_down"], **down[a])

    def multiply(yy, n):
        slab = pl.ds(pl.multiple_of(4 * yy, 4), 4)
        out = pltpu.make_async_copy(w_buf.at[slab], w_all.at[slab], here_sem.at[3 + n])
        out.start()
        here.append(out)

        def columns(b, carry):
            lanes = pl.ds(pl.multiple_of(b * 512, 512), 512)
            out = None
            for s in (0, 2):
                who = 4 * yy + s
                g = grad[:, pl.ds(pl.multiple_of(who * HEAD_DIM, 2 * HEAD_DIM), 2 * HEAD_DIM)]
                both = jnp.concatenate([w_buf[who, lanes, :], w_buf[who + 1, lanes, :]], axis=1)
                term = dot(g, both, 1, 1)
                out = term if out is None else out + term
            total[:, lanes] = out if n == 0 else total[:, lanes] + out
            return carry

        lax.fori_loop(0, total.shape[1] // 512, columns, 0)

    here.pop().wait()
    for n in (0, 3):
        to_twin[n].wait_recv()
    multiply(y, 0)

    def piece(a, who, p):
        start = pl.multiple_of(who * rows, rows) + p * (rows // 2)
        return kv.at[a, pl.ds(start, rows // 2), :]

    on_k.wait_recv()
    got = 2 * z_far + xh
    cross_k = flows.send(piece(0, got, 1), piece(0, got, 1), at["far"], **later)
    on_v.wait_recv()
    cross_v = flows.send(piece(1, got, 1), piece(1, got, 1), at["far"], **later)
    got = shard(y_far, xl, k)
    on_w0.wait_recv()
    on_s0 = flows.send(part(got, 0), part(got, 0), at["near"])
    to_twin.append(flows.send(part(got, 0), part(got, 0), at["twin"]))
    on_w1.wait_recv()
    on_s1 = flows.send(part(got, 1), part(got, 1), at["back"])
    to_twin.append(flows.send(part(got, 1), part(got, 1), at["twin"]))

    pair_up[0].wait_recv()
    got = 2 * z_down + 1 - xh
    pair_on_k = flows.send(piece(0, got, 0), piece(0, got, 0), at["z_up"], **on_up)
    pair_down[1].wait_recv()
    got = 2 * z_up + 1 - xh
    pair_on_v = flows.send(piece(1, got, 0), piece(1, got, 0), at["z_down"], **on_down)

    for p in (0, 1):
        for yy, arrived in ((y_down, side_up), (y_up, side_down)):
            got = shard(yy, 1 - xl, k)
            arrived[p].wait_recv()
            to_twin.append(flows.send(part(got, p), part(got, p), at["twin"]))
    got = shard(y_far, 1 - xl, k)
    on_s0.wait_recv()
    to_twin.append(flows.send(part(got, 0), part(got, 0), at["twin"]))
    on_s1.wait_recv()
    to_twin.append(flows.send(part(got, 1), part(got, 1), at["twin"]))
    for n in (1, 6, 8):
        to_twin[n].wait_recv()
    multiply(y_down, 1)
    for n in (2, 7, 9):
        to_twin[n].wait_recv()
    multiply(y_up, 2)
    for n in (4, 5, 10, 11):
        to_twin[n].wait_recv()
    multiply(y_far, 3)
    datt[...] = total[...].astype(BF16)
    for copy in (swap, kv_up[1], kv_down[0], pair_up[1], pair_down[0]):
        copy.wait_recv()
    for copy in (cross_k, cross_v, pair_on_k, pair_on_v):
        copy.wait_recv()
    flows.finish()
    for copy in here:
        copy.wait()


def gather(keys, values, grad, w):
    rows, kv_cols = keys.shape
    feats, cols = w.shape
    n_ctx, n_fsdp = lax.axis_size("ctx"), lax.axis_size("fsdp")
    hbm = pl.BlockSpec(memory_space=pltpu.HBM)
    vmem = pl.BlockSpec(memory_space=pltpu.VMEM)
    return pl.pallas_call(
        gather_kernel,
        in_specs=[hbm, hbm, vmem, hbm],
        out_specs=[hbm, hbm, vmem, hbm],
        out_shape=[
            jax.ShapeDtypeStruct((2, n_ctx * rows, kv_cols), BF16),
            jax.ShapeDtypeStruct((n_fsdp, feats, cols), BF16),
            jax.ShapeDtypeStruct((rows, feats), BF16),
            jax.ShapeDtypeStruct(grad.shape, BF16),
        ],
        scratch_shapes=[
            pltpu.VMEM((n_fsdp, feats, cols), BF16),
            pltpu.VMEM((rows, feats), F32),
            pltpu.SemaphoreType.DMA((GATHER_FLOWS,)),
            pltpu.SemaphoreType.DMA((GATHER_FLOWS,)),
            pltpu.SemaphoreType.DMA((7,)),
        ],
        compiler_params=pltpu.CompilerParams(
            collective_id=0, has_side_effects=True, vmem_limit_bytes=60 << 20
        ),
        cost_estimate=pl.CostEstimate(
            flops=2 * rows * feats * feats, bytes_accessed=24 << 20, transcendentals=0
        ),
        name="gather",
    )(keys, values, grad, w)


REDUCE_FLOWS = 66
PIECES = 2
PARTS = 4
PART_ROWS = 2 * HEAD_DIM // PARTS


def reduce_kernel(
    dk, dv, att, att_t, grad, grad_twin, resid, w_all,
    mixed, dk_out, dv_out, proj,
    att_twin, w_buf, res_buf, ahead, mine, hop_in, raw_in, sum_in, sum_out, kept, far_out, far_in,
    far_p, own_keep, up_raw, down_raw, top_in, low_in, top_out, low_out,
    top_raw, low_raw, top_sum, low_sum, x_out, x_in, x_keep, z_out, z_in,
    send_sem, recv_sem, here_sem,
):
    c, f, z, xh, y, xl, k = mesh_spot()
    at = neighbours()
    z_up, z_down, z_far = lax.rem(z + 1, 4), lax.rem(z + 3, 4), lax.rem(z + 2, 4)
    y_up, y_down, y_far = lax.rem(y + 1, 4), lax.rem(y + 3, 4), lax.rem(y + 2, 4)
    at["z_far"] = (2 * z_far + xh, f)
    rows, kv_cols = dk_out.shape
    pair = 2 * rows
    wide = kv_cols // PIECES
    meet(list(at.values()))
    flows = Flows(send_sem, recv_sem)
    parts = (dk, dv)

    def block(a, zz, p):
        return parts[a].at[
            pl.ds(pl.multiple_of(zz * pair, pair), pair), pl.ds(p * wide, wide)
        ]

    swap = flows.send(att_t, att_twin, at["twin"])
    hop_in_k, hop_in_v = z_down >= 2, z_up >= 2
    raw_in_k, raw_in_v = z_up >= 1, z_down == 3
    sum_in_k, sum_in_v = (z_down == 3) | (z_down == 0), z_up >= 1
    far_gives, far_takes = (z < 3) | (xh == 1), (z < 3) | (xh == 0)
    for buffer, a, comes in (
        (hop_in, 0, hop_in_k),
        (hop_in, 1, hop_in_v),
        (raw_in, 0, raw_in_k),
        (raw_in, 1, raw_in_v),
        (sum_in, 0, sum_in_k),
        (sum_in, 1, sum_in_v),
        (far_in, 0, far_takes),
        (far_in, 1, far_takes),
    ):

        def clear(buffer=buffer, a=a):
            buffer[a] = jnp.zeros_like(buffer[a])

        pl.when(jnp.logical_not(comes))(clear)
    hops = [
        [
            flows.send(block(0, z_far, p), hop_in.at[0, p], at["z_up"], z >= 2, hop_in_k),
            flows.send(block(1, z_far, p), hop_in.at[1, p], at["z_down"], z >= 2, hop_in_v),
        ]
        for p in range(PIECES)
    ]
    here = []
    for n, (src, dst) in enumerate(
        [
            (dk.at[pl.ds(pl.multiple_of(z_up * pair, pair), pair), :], ahead.at[0]),
            (dv.at[pl.ds(pl.multiple_of(z_down * pair, pair), pair), :], ahead.at[1]),
            (dk.at[pl.ds(pl.multiple_of(z * pair, pair), pair), :], mine.at[0]),
            (dv.at[pl.ds(pl.multiple_of(z * pair, pair), pair), :], mine.at[1]),
            (w_all, w_buf),
            (resid, res_buf),
        ]
    ):
        copy = pltpu.make_async_copy(src, dst, here_sem.at[n])
        copy.start()
        here.append(copy)

    def product(yy, p, low):
        lanes = [
            pl.ds(pl.multiple_of((4 * yy + 2 * s + k) * HEAD_DIM, HEAD_DIM), HEAD_DIM)
            for s in (0, 1)
        ]
        first, of = p % (PARTS // 2) * PART_ROWS, p // (PARTS // 2)

        def term(left, right):
            heads = [left[2 * (m + low) + of, first : first + PART_ROWS] for m in range(4)]
            wide = jnp.concatenate([right[:, s] for s in lanes], axis=1)
            return dot(jnp.concatenate(heads, axis=0), wide, 1, 0)

        out = term(att_t, grad) + term(att_twin, grad_twin)
        return out.reshape(4, PART_ROWS, 2 * HEAD_DIM)

    swap.wait_recv()
    top_hop, low_hop = [], []
    for p in range(PARTS):
        far_p[p, 0:4] = product(y_far, p, 0).astype(BF16)
        top_hop.append(flows.send(far_p.at[p, pl.ds(0, 4)], top_in.at[p], at["y_up"]))
        far_p[p, 4:8] = product(y_far, p, 4).astype(BF16)
        low_hop.append(flows.send(far_p.at[p, pl.ds(4, 4)], low_in.at[p], at["y_down"]))
    for copy in here[:4]:
        copy.wait()
    raws, sums = [], []
    raw_top, raw_low, top_on, low_on = [], [], [], []

    def relay_kv(p):
        cols = slice(p * wide, (p + 1) * wide)
        raws.append(
            [
                flows.send(block(0, z_down, p), raw_in.at[0, p], at["z_down"], z >= 1, raw_in_k),
                flows.send(block(1, z_up, p), raw_in.at[1, p], at["z_up"], z == 3, raw_in_v),
            ]
        )
        sums.append([])
        for a, towards, gives, takes in (
            (0, "z_up", (z == 3) | (z == 0), sum_in_k),
            (1, "z_down", z >= 1, sum_in_v),
        ):
            hops[p][a].wait_recv()
            sum_out[a, p] = (ahead[a, :, cols].astype(F32) + hop_in[a, p].astype(F32)).astype(BF16)
            sums[p].append(
                flows.send(sum_out.at[a, p], sum_in.at[a, p], at[towards], gives, takes)
            )

    for p in range(PARTS):
        up_raw[p] = product(y_up, p, 4).astype(BF16)
        raw_low.append(flows.send(up_raw.at[p], low_raw.at[p], at["y_up"]))
        down_raw[p] = product(y_down, p, 0).astype(BF16)
        raw_top.append(flows.send(down_raw.at[p], top_raw.at[p], at["y_down"]))
        keep = product(y_up, p, 0)
        top_hop[p].wait_recv()
        top_out[p] = (keep + top_in[p].astype(F32)).astype(BF16)
        top_on.append(flows.send(top_out.at[p], top_sum.at[p], at["y_up"]))
        keep = product(y_down, p, 4)
        low_hop[p].wait_recv()
        low_out[p] = (keep + low_in[p].astype(F32)).astype(BF16)
        low_on.append(flows.send(low_out.at[p], low_sum.at[p], at["y_down"]))
        if p % 2:
            relay_kv(p // 2)
    for p in range(PARTS):
        own_keep[p, 0:4] = product(y, p, 0)
        own_keep[p, 4:8] = product(y, p, 4)

    for copy in here[4:]:
        copy.wait()

    def project(n, carry):
        lanes = pl.ds(pl.multiple_of(n * 2 * HEAD_DIM, 2 * HEAD_DIM), 2 * HEAD_DIM)
        both = jnp.concatenate([w_buf[2 * n], w_buf[2 * n + 1]], axis=1)
        out = dot(att[...], both, 1, 0)
        mixed[:, lanes] = (res_buf[:, lanes].astype(F32) + out).astype(BF16)
        return carry

    def mix(quarter):
        many = w_buf.shape[0] // 8
        lax.fori_loop(quarter * many, (quarter + 1) * many, project, 0)

    keep_rows = pl.ds(pl.multiple_of(xh * rows, rows), rows)
    give_rows = pl.ds(pl.multiple_of((1 - xh) * rows, rows), rows)
    fars, x_flow, z_flow = [], [], []
    x_to = ("near", "far", "back")
    z_to = (("z_up", z_up), ("z_down", z_down), ("z_far", z_far))
    near_lanes = pl.ds(pl.multiple_of((1 - xl) * HEAD_DIM, HEAD_DIM), HEAD_DIM)
    own_lanes = pl.ds(pl.multiple_of(xl * HEAD_DIM, HEAD_DIM), HEAD_DIM)

    def cross_kv(p):
        cols = pl.ds(p * wide, wide)
        fars.append([])
        for a in (0, 1):
            raws[p][a].wait_recv()
            sums[p][a].wait_recv()

            def gathered(which):
                return (
                    mine[a, which, cols].astype(F32)
                    + raw_in[a, p, which, :].astype(F32)
                    + sum_in[a, p, which, :].astype(F32)
                )

            far_out[a, p] = gathered(give_rows).astype(BF16)
            fars[p].append(
                flows.send(far_out.at[a, p], far_in.at[a, p], at["far"], far_gives, far_takes)
            )
            kept[a, p] = gathered(keep_rows)

    def cross(p):
        raw_top[p].wait_recv()
        top_on[p].wait_recv()
        raw_low[p].wait_recv()
        low_on[p].wait_recv()
        for m in range(4):
            own_keep[p, m] += top_raw[p, m].astype(F32) + top_sum[p, m].astype(F32)
            own_keep[p, m + 4] += low_raw[p, m].astype(F32) + low_sum[p, m].astype(F32)
        sent = []
        for n, (hi, lanes) in enumerate(
            ((xh, near_lanes), (1 - xh, own_lanes), (1 - xh, near_lanes))
        ):
            for zz in range(4):
                x_out[p, n, zz] = own_keep[p, 2 * zz + hi, :, lanes].astype(BF16)
            sent.append(flows.send(x_out.at[p, n], x_in.at[p, n], at[x_to[n]]))
        x_flow.append(sent)

    def along(p):
        for n in range(3):
            x_flow[p][n].wait_recv()
        for zz in range(4):
            total = own_keep[p, 2 * zz + xh, :, own_lanes]
            for n in range(3):
                total += x_in[p, n, zz].astype(F32)
            x_keep[p, zz] = total
        sent = []
        for n, (name, zz) in enumerate(z_to):
            z_out[p, n] = x_keep[p, zz].astype(BF16)
            sent.append(flows.send(z_out.at[p, n], z_in.at[p, n], at[name]))
        z_flow.append(sent)

    def finish_kv(p):
        cols = slice(p * wide, (p + 1) * wide)
        for a, out in ((0, dk_out), (1, dv_out)):
            fars[p][a].wait_recv()
            out[:, cols] = (kept[a, p] + far_in[a, p].astype(F32)).astype(BF16)

    mix(0)
    mix(1)
    cross(0)
    cross_kv(0)
    mix(2)
    cross(1)
    along(0)
    mix(3)
    cross(2)
    along(1)
    cross_kv(1)
    finish_kv(0)
    cross(3)
    along(2)
    finish_kv(1)
    along(3)
    for p in range(PARTS):
        total = x_keep[p, z]
        for n in range(3):
            z_flow[p][n].wait_recv()
            total += z_in[p, n].astype(F32)
        proj[p * PART_ROWS : (p + 1) * PART_ROWS, :] = total
    flows.finish()


def reduce(dk, dv, att, att_t, grad, grad_twin, resid, w_all):
    n_ctx = lax.axis_size("ctx")
    seq, kv_cols = dk.shape
    rows, feats = att.shape
    chunk = seq // n_ctx
    heads = att_t.shape[0]
    per = heads // n_ctx
    wide = kv_cols // PIECES
    hbm = pl.BlockSpec(memory_space=pltpu.HBM)
    vmem = pl.BlockSpec(memory_space=pltpu.VMEM)

    def quad(dtype, n=4, lanes=2 * HEAD_DIM):
        return pltpu.VMEM((PARTS, n, PART_ROWS, lanes), dtype)

    def kv_buf(height, dtype=BF16):
        return pltpu.VMEM((2, PIECES, height, wide), dtype)

    return pl.pallas_call(
        reduce_kernel,
        in_specs=[hbm, hbm, vmem, vmem, vmem, vmem, hbm, hbm],
        out_specs=[vmem] * 4,
        out_shape=[
            jax.ShapeDtypeStruct((rows, feats), BF16),
            jax.ShapeDtypeStruct((chunk, kv_cols), BF16),
            jax.ShapeDtypeStruct((chunk, kv_cols), BF16),
            jax.ShapeDtypeStruct((per * HEAD_DIM, HEAD_DIM), F32),
        ],
        scratch_shapes=[
            pltpu.VMEM(att_t.shape, BF16),
            pltpu.VMEM(w_all.shape, BF16),
            pltpu.VMEM(resid.shape, BF16),
            pltpu.VMEM((2, 2 * chunk, kv_cols), BF16),
            pltpu.VMEM((2, 2 * chunk, kv_cols), BF16),
            kv_buf(2 * chunk),
            kv_buf(2 * chunk),
            kv_buf(2 * chunk),
            kv_buf(2 * chunk),
            kv_buf(chunk, F32),
            kv_buf(chunk),
            kv_buf(chunk),
            quad(BF16, 8),
            quad(F32, 8),
            quad(BF16),
            quad(BF16),
            quad(BF16),
            quad(BF16),
            quad(BF16),
            quad(BF16),
            quad(BF16),
            quad(BF16),
            quad(BF16),
            quad(BF16),
            pltpu.VMEM((PARTS, 3, 4, PART_ROWS, HEAD_DIM), BF16),
            pltpu.VMEM((PARTS, 3, 4, PART_ROWS, HEAD_DIM), BF16),
            quad(F32, 4, HEAD_DIM),
            quad(BF16, 3, HEAD_DIM),
            quad(BF16, 3, HEAD_DIM),
            pltpu.SemaphoreType.DMA((REDUCE_FLOWS,)),
            pltpu.SemaphoreType.DMA((REDUCE_FLOWS,)),
            pltpu.SemaphoreType.DMA((6,)),
        ],
        compiler_params=pltpu.CompilerParams(
            collective_id=1, has_side_effects=True, vmem_limit_bytes=40 << 20
        ),
        cost_estimate=pl.CostEstimate(
            flops=4 * rows * feats * feats, bytes_accessed=24 << 20, transcendentals=0
        ),
        name="reduce",
    )(dk, dv, att, att_t, grad, grad_twin, resid, w_all)


def local(queries, keys, values, resid, grad_out, w_out, block_list, block_count):
    grad = grad_out[0]
    kv, w_all, datt, grad_twin = gather(keys[0], values[0], grad, w_out)
    att, att_t, dq, dk, dv = attention(queries[0], datt, kv, block_list, block_count)
    mixed, dk, dv, proj = reduce(dk, dv, att, att_t, grad, grad_twin, resid[0], w_all)
    return mixed[None], dq[None], dk[None], dv[None], proj


def solution(mesh):
    rows = P("fsdp", "ctx", None)
    in_specs = (rows, rows, rows, rows, rows, P(None, "fsdp"), P("ctx", None), P("ctx"))
    out_specs = (rows, rows, rows, rows, P("ctx", "fsdp"))
    return jax.shard_map(local, mesh=mesh, in_specs=in_specs, out_specs=out_specs, check_vma=False)
```

```python
import functools
import itertools
import math

import jax
import jax.numpy as jnp
from jax import lax
from jax.experimental import pallas as pl
from jax.experimental.pallas import tpu as pltpu
from jax.sharding import PartitionSpec as P

QUERY_HEADS = 16
KV_HEADS = 4
GROUP = QUERY_HEADS // KV_HEADS
HEAD_DIM = 128
BLOCK = 128
SLOTS = 8
STEP = 4
SCALE = 1.0 / math.sqrt(HEAD_DIM)
BF16 = jnp.bfloat16
F32 = jnp.float32
LOG2E = math.log2(math.e)
MESH = pl.DeviceIdType.MESH


def dot(a, b, ca, cb):
    return lax.dot_general(a, b, (((ca,), (cb,)), ((), ())), preferred_element_type=F32)


def stack_heads(ref, i):
    rows = slice(i * BLOCK, (i + 1) * BLOCK)
    return jnp.concatenate(
        [ref[rows, h * HEAD_DIM : (h + 1) * HEAD_DIM] for h in range(GROUP)], axis=0
    )


def attention_kernel(
    list_ref, count_ref, q_ref, do_ref, k_ref, v_ref,
    att_ref, att_t_ref, dq_ref, dk_ref, dv_ref, dk_acc, dv_acc,
):
    cols = GROUP * BLOCK
    count = q_ref.shape[0] // BLOCK
    dk_acc[...] = jnp.zeros_like(dk_acc)
    dv_acc[...] = jnp.zeros_like(dv_acc)

    def slots(ns):
        key_pos = lax.broadcasted_iota(jnp.int32, (BLOCK, cols), 0)
        query_pos = lax.broadcasted_iota(jnp.int32, (BLOCK, cols), 1) % BLOCK
        rows, k_sel, v_sel, qs, dos = [], [], [], [], []
        for i, n in enumerate(ns):
            rows.append(
                [pl.ds(pl.multiple_of(list_ref[i, j] * BLOCK, BLOCK), BLOCK) for j in range(n)]
            )
            k_sel.append(jnp.concatenate([k_ref[0, r, :] for r in rows[i]], axis=0))
            v_sel.append(jnp.concatenate([v_ref[0, r, :] for r in rows[i]], axis=0))
            qs.append(stack_heads(q_ref, i))
            dos.append(stack_heads(do_ref, i))
        scores = [dot(k, q, 1, 1) for k, q in zip(k_sel, qs)]
        prob_grads = [dot(v, do, 1, 1) for v, do in zip(v_sel, dos)]
        probs, rounded = [], []
        for i, (s, n) in enumerate(zip(scores, ns)):
            parts = [jnp.where(key_pos <= query_pos, s[:BLOCK], -1e30)]
            if n > STEP:
                parts.append(s[BLOCK : (n - STEP + 1) * BLOCK])
            for j in range(n - STEP + 1, n):
                dead = jnp.where(j < count_ref[i], 0.0, -1e30).astype(F32)
                parts.append(s[j * BLOCK : (j + 1) * BLOCK] + dead)
            s = jnp.concatenate(parts, axis=0)
            top = jnp.max(s, axis=0, keepdims=True)
            e = jnp.exp2((s - top) * (SCALE * LOG2E))
            p = e * (1.0 / jnp.sum(e, axis=0, keepdims=True))
            probs.append(p)
            rounded.append(p.astype(BF16))
        outs = [dot(v, pb, 0, 0).astype(BF16) for v, pb in zip(v_sel, rounded)]
        row_dots = [
            jnp.sum(o.astype(F32) * do.T.astype(F32), axis=0, keepdims=True)
            for o, do in zip(outs, dos)
        ]
        grads = [
            (p * (dp - r)).astype(BF16) for p, dp, r in zip(probs, prob_grads, row_dots)
        ]
        dqs = [(dot(k, ds, 0, 0) * SCALE).astype(BF16).T for k, ds in zip(k_sel, grads)]
        dks = [dot(ds, q, 1, 0) for ds, q in zip(grads, qs)]
        dvs = [dot(pb, do, 1, 0) for pb, do in zip(rounded, dos)]
        for i, (o_t, dq) in enumerate(zip(outs, dqs)):
            o = o_t.T
            mine = slice(i * BLOCK, (i + 1) * BLOCK)
            for h in range(GROUP):
                lanes = slice(h * HEAD_DIM, (h + 1) * HEAD_DIM)
                here = slice(h * BLOCK, (h + 1) * BLOCK)
                att_ref[mine, lanes] = o[here]
                dq_ref[mine, lanes] = dq[here]
                att_t_ref[h, :, mine] = o_t[:, here]
        for i, n in enumerate(ns):
            for j in range(n):
                here = slice(j * BLOCK, (j + 1) * BLOCK)
                dk_acc[rows[i][j], :] += dks[i][here]
                dv_acc[rows[i][j], :] += dvs[i][here]

    need = [(count_ref[i] + STEP - 1) // STEP for i in range(count)]
    for ns in itertools.product(range(STEP, SLOTS + 1, STEP), repeat=count):
        hit = functools.reduce(
            jnp.logical_and, [have == n // STEP for have, n in zip(need, ns)]
        )
        pl.when(hit)(functools.partial(slots, ns))

    dk_ref[...] = (dk_acc[...] * SCALE).astype(BF16)
    dv_ref[...] = dv_acc[...].astype(BF16)


def attention(queries, datt, kv, block_list, block_count):
    rows, width = queries.shape
    seq = kv.shape[1]
    group_cols = GROUP * HEAD_DIM
    kv_cols = KV_HEADS * HEAD_DIM
    q_spec = pl.BlockSpec((rows, group_cols), lambda g, *_: (0, g))

    def kv_spec(which):
        return pl.BlockSpec((1, seq, HEAD_DIM), lambda g, *_: (which, 0, g))

    out_spec = pl.BlockSpec((seq, HEAD_DIM), lambda g, *_: (0, g))
    t_spec = pl.BlockSpec((GROUP, HEAD_DIM, rows), lambda g, *_: (g, 0, 0))
    flops = 12 * rows * QUERY_HEADS * SLOTS * BLOCK * HEAD_DIM
    return pl.pallas_call(
        attention_kernel,
        grid_spec=pltpu.PrefetchScalarGridSpec(
            num_scalar_prefetch=2,
            grid=(KV_HEADS,),
            in_specs=[q_spec, q_spec, kv_spec(0), kv_spec(1)],
            out_specs=[q_spec, t_spec, q_spec, out_spec, out_spec],
            scratch_shapes=[pltpu.VMEM((seq, HEAD_DIM), F32)] * 2,
        ),
        out_shape=[
            jax.ShapeDtypeStruct((rows, width), BF16),
            jax.ShapeDtypeStruct((QUERY_HEADS, HEAD_DIM, rows), BF16),
            jax.ShapeDtypeStruct((rows, width), BF16),
            jax.ShapeDtypeStruct((seq, kv_cols), BF16),
            jax.ShapeDtypeStruct((seq, kv_cols), BF16),
        ],
        compiler_params=pltpu.CompilerParams(
            dimension_semantics=("arbitrary",), vmem_limit_bytes=44 << 20
        ),
        cost_estimate=pl.CostEstimate(
            flops=flops, bytes_accessed=12 << 20, transcendentals=rows * QUERY_HEADS * SLOTS * BLOCK
        ),
        name="attention",
    )(block_list, block_count, queries, datt, kv, kv)


def mesh_spot():
    c, f = lax.axis_index("ctx"), lax.axis_index("fsdp")
    return c, f, c // 2, lax.rem(c, 2), f // 4, lax.rem(f // 2, 2), lax.rem(f, 2)


def neighbours():
    c, f, z, xh, y, xl, k = mesh_spot()
    z_up, z_down = lax.rem(z + 1, 4), lax.rem(z + 3, 4)
    y_up, y_down = lax.rem(y + 1, 4), lax.rem(y + 3, 4)
    side, far, twin = 4 * y + 2 * (1 - xl) + k, 2 * z + 1 - xh, 4 * y + 2 * xl + 1 - k
    return dict(
        far=(far, f),
        near=(c, side),
        back=(far, side),
        twin=(c, twin),
        z_up=(2 * z_up + xh, f),
        z_down=(2 * z_down + xh, f),
        y_up=(c, 4 * y_up + 2 * xl + k),
        y_down=(c, 4 * y_down + 2 * xl + k),
    )


def meet(peers):
    barrier = pltpu.get_barrier_semaphore()
    for peer in peers:
        pl.semaphore_signal(barrier, inc=1, device_id=peer, device_id_type=MESH)
    pl.semaphore_wait(barrier, len(peers))


def act_if(condition, act):
    def run():
        act()

    if condition is None:
        run()
    else:
        pl.when(condition)(run)


class Sent:
    def __init__(self, copy, gives, takes):
        self.copy, self.gives, self.takes = copy, gives, takes

    def wait_recv(self):
        act_if(self.takes, self.copy.wait_recv)

    def wait_send(self):
        act_if(self.gives, self.copy.wait_send)


class Flows:
    def __init__(self, send_sem, recv_sem):
        self.send_sem, self.recv_sem, self.made = send_sem, recv_sem, []

    def send(self, src, dst, peer, gives=None, takes=None):
        n = len(self.made)
        copy = pltpu.make_async_remote_copy(
            src_ref=src,
            dst_ref=dst,
            send_sem=self.send_sem.at[n],
            recv_sem=self.recv_sem.at[n],
            device_id=peer,
            device_id_type=MESH,
        )
        act_if(gives, copy.start)
        self.made.append(Sent(copy, gives, takes))
        return self.made[-1]

    def finish(self):
        for copy in self.made:
            copy.wait_send()


GATHER_FLOWS = 40


def gather_kernel(
    keys, values, grad, w, kv, w_all, datt, grad_twin, w_buf, total, send_sem, recv_sem, here_sem
):
    c, f, z, xh, y, xl, k = mesh_spot()
    at = neighbours()
    z_up, z_down, z_far = lax.rem(z + 1, 4), lax.rem(z + 3, 4), lax.rem(z + 2, 4)
    y_up, y_down, y_far = lax.rem(y + 1, 4), lax.rem(y + 3, 4), lax.rem(y + 2, 4)
    rows = keys.shape[0]
    half = w.shape[0] // 2
    meet(list(at.values()))
    flows = Flows(send_sem, recv_sem)

    def chunk(a, who):
        return kv.at[a, pl.ds(pl.multiple_of(who * rows, rows), rows), :]

    def shard(yy, xx, kk):
        return 4 * yy + 2 * xx + kk

    def whole(who):
        return w_buf.at[who]

    def part(who, p):
        return w_buf.at[who, pl.ds(p * half, half), :]

    own = (keys, values)
    up = dict(gives=z < 3, takes=z_down < 3)
    down = (dict(gives=z < 1, takes=z_up < 1), dict(gives=z < 2, takes=z_up < 2))
    on_up = dict(gives=(z == 1) | (z == 2), takes=z >= 2)
    on_down = dict(gives=(z == 0) | (z == 3), takes=z >= 2)
    later = dict(gives=z >= 2, takes=z >= 2)
    w_side = [
        flows.send(w.at[pl.ds(p * half, half), :], part(f, p), at[("near", "back")[p]])
        for p in (0, 1)
    ]
    w_up = flows.send(w, whole(f), at["y_up"])
    w_down = flows.send(w, whole(f), at["y_down"])
    kv_up = [flows.send(own[a], chunk(a, c), at["z_up"], **up) for a in (0, 1)]
    kv_down = [flows.send(own[a], chunk(a, c), at["z_down"], **down[a]) for a in (1, 0)][::-1]
    kv_far = [flows.send(own[a], chunk(a, c), at["far"]) for a in (0, 1)]
    to_twin = [flows.send(w, whole(f), at["twin"])]
    swap = flows.send(grad, grad_twin, at["twin"])
    here = [
        pltpu.make_async_copy(keys, chunk(0, c), here_sem.at[0]),
        pltpu.make_async_copy(values, chunk(1, c), here_sem.at[1]),
        pltpu.make_async_copy(w, whole(f), here_sem.at[2]),
    ]
    for copy in here:
        copy.start()

    side = shard(y, 1 - xl, k)
    side_up, side_down = [], []

    def pass_side(p):
        w_side[p].wait_recv()
        side_up.append(flows.send(part(side, p), part(side, p), at["y_up"]))
        side_down.append(flows.send(part(side, p), part(side, p), at["y_down"]))

    pass_side(0)
    kv_up[0].wait_recv()
    got_k = 2 * z_down + xh
    on_k = flows.send(chunk(0, got_k), chunk(0, got_k), at["z_up"], **on_up)
    kv_down[1].wait_recv()
    got_v = 2 * z_up + xh
    on_v = flows.send(chunk(1, got_v), chunk(1, got_v), at["z_down"], **on_down)
    w_up.wait_recv()
    got = shard(y_down, xl, k)
    on_w0 = flows.send(part(got, 0), part(got, 0), at["y_up"])
    to_twin.append(flows.send(whole(got), whole(got), at["twin"]))
    w_down.wait_recv()
    got = shard(y_up, xl, k)
    on_w1 = flows.send(part(got, 1), part(got, 1), at["y_down"])
    to_twin.append(flows.send(whole(got), whole(got), at["twin"]))
    pass_side(1)
    to_twin.append(flows.send(whole(side), whole(side), at["twin"]))

    other = 2 * z + 1 - xh
    pair_up, pair_down = [None, None], [None, None]
    for a in (0, 1):
        kv_far[a].wait_recv()
        pair_up[a] = flows.send(chunk(a, other), chunk(a, other), at["z_up"], **up)
        pair_down[a] = flows.send(chunk(a, other), chunk(a, other), at["z_down"], **down[a])

    def multiply(yy, n):
        slab = pl.ds(pl.multiple_of(4 * yy, 4), 4)
        out = pltpu.make_async_copy(w_buf.at[slab], w_all.at[slab], here_sem.at[3 + n])
        out.start()
        here.append(out)

        def columns(b, carry):
            lanes = pl.ds(pl.multiple_of(b * 512, 512), 512)
            out = None
            for s in (0, 2):
                who = 4 * yy + s
                g = grad[:, pl.ds(pl.multiple_of(who * HEAD_DIM, 2 * HEAD_DIM), 2 * HEAD_DIM)]
                both = jnp.concatenate([w_buf[who, lanes, :], w_buf[who + 1, lanes, :]], axis=1)
                term = dot(g, both, 1, 1)
                out = term if out is None else out + term
            total[:, lanes] = out if n == 0 else total[:, lanes] + out
            return carry

        lax.fori_loop(0, total.shape[1] // 512, columns, 0)

    here.pop().wait()
    for n in (0, 3):
        to_twin[n].wait_recv()
    multiply(y, 0)

    def piece(a, who, p):
        start = pl.multiple_of(who * rows, rows) + p * (rows // 2)
        return kv.at[a, pl.ds(start, rows // 2), :]

    on_k.wait_recv()
    got = 2 * z_far + xh
    cross_k = flows.send(piece(0, got, 1), piece(0, got, 1), at["far"], **later)
    on_v.wait_recv()
    cross_v = flows.send(piece(1, got, 1), piece(1, got, 1), at["far"], **later)
    got = shard(y_far, xl, k)
    on_w0.wait_recv()
    on_s0 = flows.send(part(got, 0), part(got, 0), at["near"])
    to_twin.append(flows.send(part(got, 0), part(got, 0), at["twin"]))
    on_w1.wait_recv()
    on_s1 = flows.send(part(got, 1), part(got, 1), at["back"])
    to_twin.append(flows.send(part(got, 1), part(got, 1), at["twin"]))

    pair_up[0].wait_recv()
    got = 2 * z_down + 1 - xh
    pair_on_k = flows.send(piece(0, got, 0), piece(0, got, 0), at["z_up"], **on_up)
    pair_down[1].wait_recv()
    got = 2 * z_up + 1 - xh
    pair_on_v = flows.send(piece(1, got, 0), piece(1, got, 0), at["z_down"], **on_down)

    for yy, arrived in ((y_down, side_up), (y_up, side_down)):
        got = shard(yy, 1 - xl, k)
        for copy in arrived:
            copy.wait_recv()
        to_twin.append(flows.send(whole(got), whole(got), at["twin"]))
    got = shard(y_far, 1 - xl, k)
    on_s0.wait_recv()
    to_twin.append(flows.send(part(got, 0), part(got, 0), at["twin"]))
    on_s1.wait_recv()
    to_twin.append(flows.send(part(got, 1), part(got, 1), at["twin"]))
    for n in (1, 6):
        to_twin[n].wait_recv()
    multiply(y_down, 1)
    for n in (2, 7):
        to_twin[n].wait_recv()
    multiply(y_up, 2)
    for n in (4, 5, 8, 9):
        to_twin[n].wait_recv()
    multiply(y_far, 3)
    datt[...] = total[...].astype(BF16)
    for copy in (swap, kv_up[1], kv_down[0], pair_up[1], pair_down[0]):
        copy.wait_recv()
    for copy in (cross_k, cross_v, pair_on_k, pair_on_v):
        copy.wait_recv()
    flows.finish()
    for copy in here:
        copy.wait()


def gather(keys, values, grad, w):
    rows, kv_cols = keys.shape
    feats, cols = w.shape
    n_ctx, n_fsdp = lax.axis_size("ctx"), lax.axis_size("fsdp")
    hbm = pl.BlockSpec(memory_space=pltpu.HBM)
    vmem = pl.BlockSpec(memory_space=pltpu.VMEM)
    return pl.pallas_call(
        gather_kernel,
        in_specs=[hbm, hbm, vmem, hbm],
        out_specs=[hbm, hbm, vmem, hbm],
        out_shape=[
            jax.ShapeDtypeStruct((2, n_ctx * rows, kv_cols), BF16),
            jax.ShapeDtypeStruct((n_fsdp, feats, cols), BF16),
            jax.ShapeDtypeStruct((rows, feats), BF16),
            jax.ShapeDtypeStruct(grad.shape, BF16),
        ],
        scratch_shapes=[
            pltpu.VMEM((n_fsdp, feats, cols), BF16),
            pltpu.VMEM((rows, feats), F32),
            pltpu.SemaphoreType.DMA((GATHER_FLOWS,)),
            pltpu.SemaphoreType.DMA((GATHER_FLOWS,)),
            pltpu.SemaphoreType.DMA((7,)),
        ],
        compiler_params=pltpu.CompilerParams(
            collective_id=0, has_side_effects=True, vmem_limit_bytes=60 << 20
        ),
        cost_estimate=pl.CostEstimate(
            flops=2 * rows * feats * feats, bytes_accessed=24 << 20, transcendentals=0
        ),
        name="gather",
    )(keys, values, grad, w)


REDUCE_FLOWS = 66
PIECES = 2
PARTS = 4
PART_ROWS = 2 * HEAD_DIM // PARTS


def reduce_kernel(
    dk, dv, att, att_t, grad, grad_twin, resid, w_all,
    mixed, dk_out, dv_out, proj,
    att_twin, w_buf, res_buf, ahead, mine, hop_in, raw_in, sum_in, sum_out, kept, far_out, far_in,
    far_p, own_keep, up_raw, down_raw, top_in, low_in, top_out, low_out,
    top_raw, low_raw, top_sum, low_sum, x_out, x_in, x_keep, z_out, z_in,
    send_sem, recv_sem, here_sem,
):
    c, f, z, xh, y, xl, k = mesh_spot()
    at = neighbours()
    z_up, z_down, z_far = lax.rem(z + 1, 4), lax.rem(z + 3, 4), lax.rem(z + 2, 4)
    y_up, y_down, y_far = lax.rem(y + 1, 4), lax.rem(y + 3, 4), lax.rem(y + 2, 4)
    at["z_far"] = (2 * z_far + xh, f)
    rows, kv_cols = dk_out.shape
    pair = 2 * rows
    wide = kv_cols // PIECES
    meet(list(at.values()))
    flows = Flows(send_sem, recv_sem)
    parts = (dk, dv)

    def block(a, zz, p):
        return parts[a].at[
            pl.ds(pl.multiple_of(zz * pair, pair), pair), pl.ds(p * wide, wide)
        ]

    stripes = [pl.ds(n * PART_ROWS, PART_ROWS) for n in range(PARTS // 2)]
    swaps = [
        flows.send(att_t.at[:, s, :], att_twin.at[:, s, :], at["twin"]) for s in stripes
    ]
    hop_in_k, hop_in_v = z_down >= 2, z_up >= 2
    raw_in_k, raw_in_v = z_up >= 1, z_down == 3
    sum_in_k, sum_in_v = (z_down == 3) | (z_down == 0), z_up >= 1
    for buffer, a, comes in (
        (hop_in, 0, hop_in_k),
        (hop_in, 1, hop_in_v),
        (raw_in, 0, raw_in_k),
        (raw_in, 1, raw_in_v),
        (sum_in, 0, sum_in_k),
        (sum_in, 1, sum_in_v),
    ):

        def clear(buffer=buffer, a=a):
            buffer[a] = jnp.zeros_like(buffer[a])

        pl.when(jnp.logical_not(comes))(clear)
    hops = [
        [
            flows.send(block(0, z_far, p), hop_in.at[0, p], at["z_up"], z >= 2, hop_in_k),
            flows.send(block(1, z_far, p), hop_in.at[1, p], at["z_down"], z >= 2, hop_in_v),
        ]
        for p in range(PIECES)
    ]
    here = []
    for n, (src, dst) in enumerate(
        [
            (dk.at[pl.ds(pl.multiple_of(z_up * pair, pair), pair), :], ahead.at[0]),
            (dv.at[pl.ds(pl.multiple_of(z_down * pair, pair), pair), :], ahead.at[1]),
            (dk.at[pl.ds(pl.multiple_of(z * pair, pair), pair), :], mine.at[0]),
            (dv.at[pl.ds(pl.multiple_of(z * pair, pair), pair), :], mine.at[1]),
            (w_all, w_buf),
            (resid, res_buf),
        ]
    ):
        copy = pltpu.make_async_copy(src, dst, here_sem.at[n])
        if n < 4:
            copy.start()
        here.append(copy)

    def product(yy, p, low):
        lanes = [
            pl.ds(pl.multiple_of((4 * yy + 2 * s + k) * HEAD_DIM, HEAD_DIM), HEAD_DIM)
            for s in (0, 1)
        ]
        first, of = p % (PARTS // 2) * PART_ROWS, p // (PARTS // 2)

        def term(left, right):
            heads = [left[2 * (m + low) + of, first : first + PART_ROWS] for m in range(4)]
            wide = jnp.concatenate([right[:, s] for s in lanes], axis=1)
            return dot(jnp.concatenate(heads, axis=0), wide, 1, 0)

        out = term(att_t, grad) + term(att_twin, grad_twin)
        return out.reshape(4, PART_ROWS, 2 * HEAD_DIM)

    top_hop, low_hop = [], []
    for p in range(PARTS):
        if p < len(swaps):
            swaps[p].wait_recv()
        far_p[p, 0:4] = product(y_far, p, 0).astype(BF16)
        top_hop.append(flows.send(far_p.at[p, pl.ds(0, 4)], top_in.at[p], at["y_up"]))
        far_p[p, 4:8] = product(y_far, p, 4).astype(BF16)
        low_hop.append(flows.send(far_p.at[p, pl.ds(4, 4)], low_in.at[p], at["y_down"]))
    for copy in here[:4]:
        copy.wait()
    raws, sums = [], []
    raw_top, raw_low, top_on, low_on = [], [], [], []

    def relay_kv(p):
        cols = slice(p * wide, (p + 1) * wide)
        raws.append(
            [
                flows.send(block(0, z_down, p), raw_in.at[0, p], at["z_down"], z >= 1, raw_in_k),
                flows.send(block(1, z_up, p), raw_in.at[1, p], at["z_up"], z == 3, raw_in_v),
            ]
        )
        sums.append([])
        for a, towards, gives, takes in (
            (0, "z_up", (z == 3) | (z == 0), sum_in_k),
            (1, "z_down", z >= 1, sum_in_v),
        ):
            hops[p][a].wait_recv()
            sum_out[a, p] = (ahead[a, :, cols].astype(F32) + hop_in[a, p].astype(F32)).astype(BF16)
            sums[p].append(
                flows.send(sum_out.at[a, p], sum_in.at[a, p], at[towards], gives, takes)
            )

    for p in range(PARTS):
        up_raw[p] = product(y_up, p, 4).astype(BF16)
        raw_low.append(flows.send(up_raw.at[p], low_raw.at[p], at["y_up"]))
        down_raw[p] = product(y_down, p, 0).astype(BF16)
        raw_top.append(flows.send(down_raw.at[p], top_raw.at[p], at["y_down"]))
        keep = product(y_up, p, 0)
        top_hop[p].wait_recv()
        top_out[p] = (keep + top_in[p].astype(F32)).astype(BF16)
        top_on.append(flows.send(top_out.at[p], top_sum.at[p], at["y_up"]))
        keep = product(y_down, p, 4)
        low_hop[p].wait_recv()
        low_out[p] = (keep + low_in[p].astype(F32)).astype(BF16)
        low_on.append(flows.send(low_out.at[p], low_sum.at[p], at["y_down"]))
        if p % 2:
            relay_kv(p // 2)
            here[4 + p // 2].start()
    for p in range(PARTS):
        own_keep[p, 0:4] = product(y, p, 0)
        own_keep[p, 4:8] = product(y, p, 4)

    for copy in here[4:]:
        copy.wait()

    def project(n, carry):
        lanes = pl.ds(pl.multiple_of(n * 2 * HEAD_DIM, 2 * HEAD_DIM), 2 * HEAD_DIM)
        both = jnp.concatenate([w_buf[2 * n], w_buf[2 * n + 1]], axis=1)
        out = dot(att[...], both, 1, 0)
        mixed[:, lanes] = (res_buf[:, lanes].astype(F32) + out).astype(BF16)
        return carry

    def mix(quarter):
        many = w_buf.shape[0] // 8
        lax.fori_loop(quarter * many, (quarter + 1) * many, project, 0)

    keep_rows = pl.ds(pl.multiple_of(xh * rows, rows), rows)
    give_rows = pl.ds(pl.multiple_of((1 - xh) * rows, rows), rows)
    fars, x_flow, z_flow = [], [], []
    x_to = ("near", "far", "back")
    z_to = (("z_up", z_up), ("z_down", z_down), ("z_far", z_far))
    near_lanes = pl.ds(pl.multiple_of((1 - xl) * HEAD_DIM, HEAD_DIM), HEAD_DIM)
    own_lanes = pl.ds(pl.multiple_of(xl * HEAD_DIM, HEAD_DIM), HEAD_DIM)

    def cross_kv(p):
        cols = pl.ds(p * wide, wide)
        fars.append([])
        for a in (0, 1):
            raws[p][a].wait_recv()
            sums[p][a].wait_recv()

            def gathered(which):
                return (
                    mine[a, which, cols].astype(F32)
                    + raw_in[a, p, which, :].astype(F32)
                    + sum_in[a, p, which, :].astype(F32)
                )

            far_out[a, p] = gathered(give_rows).astype(BF16)
            fars[p].append(flows.send(far_out.at[a, p], far_in.at[a, p], at["far"]))
            kept[a, p] = gathered(keep_rows)

    def cross(p):
        raw_top[p].wait_recv()
        top_on[p].wait_recv()
        raw_low[p].wait_recv()
        low_on[p].wait_recv()
        for m in range(4):
            own_keep[p, m] += top_raw[p, m].astype(F32) + top_sum[p, m].astype(F32)
            own_keep[p, m + 4] += low_raw[p, m].astype(F32) + low_sum[p, m].astype(F32)
        sent = []
        for n, (hi, lanes) in enumerate(
            ((xh, near_lanes), (1 - xh, own_lanes), (1 - xh, near_lanes))
        ):
            for zz in range(4):
                x_out[p, n, zz] = own_keep[p, 2 * zz + hi, :, lanes].astype(BF16)
            sent.append(flows.send(x_out.at[p, n], x_in.at[p, n], at[x_to[n]]))
        x_flow.append(sent)

    def along(p):
        for n in range(3):
            x_flow[p][n].wait_recv()
        for zz in range(4):
            total = own_keep[p, 2 * zz + xh, :, own_lanes]
            for n in range(3):
                total += x_in[p, n, zz].astype(F32)
            x_keep[p, zz] = total
        sent = []
        for n, (name, zz) in enumerate(z_to):
            z_out[p, n] = x_keep[p, zz].astype(BF16)
            sent.append(flows.send(z_out.at[p, n], z_in.at[p, n], at[name]))
        z_flow.append(sent)

    def finish_kv(p):
        cols = slice(p * wide, (p + 1) * wide)
        for a, out in ((0, dk_out), (1, dv_out)):
            fars[p][a].wait_recv()
            out[:, cols] = (kept[a, p] + far_in[a, p].astype(F32)).astype(BF16)

    mix(0)
    mix(1)
    cross(0)
    cross_kv(0)
    mix(2)
    cross(1)
    along(0)
    mix(3)
    cross(2)
    along(1)
    cross_kv(1)
    finish_kv(0)
    cross(3)
    along(2)
    finish_kv(1)
    along(3)
    for p in range(PARTS):
        total = x_keep[p, z]
        for n in range(3):
            z_flow[p][n].wait_recv()
            total += z_in[p, n].astype(F32)
        proj[p * PART_ROWS : (p + 1) * PART_ROWS, :] = total
    flows.finish()


def reduce(dk, dv, att, att_t, grad, grad_twin, resid, w_all):
    n_ctx = lax.axis_size("ctx")
    seq, kv_cols = dk.shape
    rows, feats = att.shape
    chunk = seq // n_ctx
    heads = att_t.shape[0]
    per = heads // n_ctx
    wide = kv_cols // PIECES
    hbm = pl.BlockSpec(memory_space=pltpu.HBM)
    vmem = pl.BlockSpec(memory_space=pltpu.VMEM)

    def quad(dtype, n=4, lanes=2 * HEAD_DIM):
        return pltpu.VMEM((PARTS, n, PART_ROWS, lanes), dtype)

    def kv_buf(height, dtype=BF16):
        return pltpu.VMEM((2, PIECES, height, wide), dtype)

    return pl.pallas_call(
        reduce_kernel,
        in_specs=[hbm, hbm, vmem, vmem, vmem, vmem, hbm, hbm],
        out_specs=[vmem] * 4,
        out_shape=[
            jax.ShapeDtypeStruct((rows, feats), BF16),
            jax.ShapeDtypeStruct((chunk, kv_cols), BF16),
            jax.ShapeDtypeStruct((chunk, kv_cols), BF16),
            jax.ShapeDtypeStruct((per * HEAD_DIM, HEAD_DIM), F32),
        ],
        scratch_shapes=[
            pltpu.VMEM(att_t.shape, BF16),
            pltpu.VMEM(w_all.shape, BF16),
            pltpu.VMEM(resid.shape, BF16),
            pltpu.VMEM((2, 2 * chunk, kv_cols), BF16),
            pltpu.VMEM((2, 2 * chunk, kv_cols), BF16),
            kv_buf(2 * chunk),
            kv_buf(2 * chunk),
            kv_buf(2 * chunk),
            kv_buf(2 * chunk),
            kv_buf(chunk, F32),
            kv_buf(chunk),
            kv_buf(chunk),
            quad(BF16, 8),
            quad(F32, 8),
            quad(BF16),
            quad(BF16),
            quad(BF16),
            quad(BF16),
            quad(BF16),
            quad(BF16),
            quad(BF16),
            quad(BF16),
            quad(BF16),
            quad(BF16),
            pltpu.VMEM((PARTS, 3, 4, PART_ROWS, HEAD_DIM), BF16),
            pltpu.VMEM((PARTS, 3, 4, PART_ROWS, HEAD_DIM), BF16),
            quad(F32, 4, HEAD_DIM),
            quad(BF16, 3, HEAD_DIM),
            quad(BF16, 3, HEAD_DIM),
            pltpu.SemaphoreType.DMA((REDUCE_FLOWS,)),
            pltpu.SemaphoreType.DMA((REDUCE_FLOWS,)),
            pltpu.SemaphoreType.DMA((6,)),
        ],
        compiler_params=pltpu.CompilerParams(
            collective_id=1, has_side_effects=True, vmem_limit_bytes=40 << 20
        ),
        cost_estimate=pl.CostEstimate(
            flops=4 * rows * feats * feats, bytes_accessed=24 << 20, transcendentals=0
        ),
        name="reduce",
    )(dk, dv, att, att_t, grad, grad_twin, resid, w_all)


def local(queries, keys, values, resid, grad_out, w_out, block_list, block_count):
    grad = grad_out[0]
    kv, w_all, datt, grad_twin = gather(keys[0], values[0], grad, w_out)
    att, att_t, dq, dk, dv = attention(queries[0], datt, kv, block_list, block_count)
    mixed, dk, dv, proj = reduce(dk, dv, att, att_t, grad, grad_twin, resid[0], w_all)
    return mixed[None], dq[None], dk[None], dv[None], proj


def solution(mesh):
    rows = P("fsdp", "ctx", None)
    in_specs = (rows, rows, rows, rows, rows, P(None, "fsdp"), P("ctx", None), P("ctx"))
    out_specs = (rows, rows, rows, rows, P("ctx", "fsdp"))
    return jax.shard_map(local, mesh=mesh, in_specs=in_specs, out_specs=out_specs, check_vma=False)
```
